32 devices in a mesh: dp: 8 (over z, core), graph: 4 (over y, x).
Axes of the slice: x: 2, y: 2, z: 4, core: 2. Of those that a mesh axis runs over, the one named last changes fastest.
Arguments:
- edge_feats: bfloat16 [32768, 512], P(('dp', 'graph')), may hold values from -6 to 6
- cotangent: bfloat16 [32768, 512], P(('dp', 'graph')), may hold values from -6 to 6
- angle_basis: bfloat16 [16, 262144], P(None, ('dp', 'graph')), may hold values from -6 to 6
- source_edge: int32 [262144], P(('dp', 'graph')), may hold values from 0 to 4095
- target_edge: int32 [262144], P(('dp', 'graph')), may hold values from 0 to 1023
- pair_weight: bfloat16 [512, 512], P('dp'), may hold values from -0.25 to 0.25
- down_weight: bfloat16 [512, 64], P('dp'), may hold values from -0.25 to 0.25
- basis_weight: bfloat16 [16, 64], P('dp'), may hold values from -1.5 to 1.5
- up_weight: bfloat16 [64, 512], P('dp'), may hold values from -0.75 to 0.75
- res_first: bfloat16 [512, 512], P('dp'), may hold values from -0.25 to 0.25
- res_second: bfloat16 [512, 512], P('dp'), may hold values from -0.25 to 0.25
Outputs:
- edge_grad: bfloat16 [32768, 512], P(('dp', 'graph'))
- pair_grad: float32 [512, 512], P('dp')
- down_grad: float32 [512, 64], P('dp')
- basis_grad: float32 [16, 64], P('dp')
- up_grad: float32 [64, 512], P('dp')
- first_grad: float32 [512, 512], P('dp')
- second_grad: float32 [512, 512], P('dp')
The draws below stay inside these ranges and needn't reach their ends.
Inputs may be any that keep to these rules, and one draw needn't show every extreme that they name: source_edge[t] may name any edge of the 4 devices of the triplet's group. target_edge[t] names an edge of the triplet's own device.
All inputs are finite; a program needn't handle non-finite values.
Results may differ from the reference program's by a relative error of at most 0.013.
Values may be sent and summed in bfloat16 or wider, within the bound.
A program may use at most 64 MiB of HBM per device.

```python
import math
import jax
import jax.numpy as jnp
from jax import lax

D = 512
DT = 64
NCBF = 16
E_DEV = 1024
T_DEV = 8192
E_GRP = 4096
T_GRP = 32768
EDGES = 32768
TRIPS = 262144
N_DP = 8


def set_ends(entries, key, smallest, high):
    shape = entries.shape
    index_at = [jax.random.randint(jax.random.fold_in(key, axis), (), 0, shape[axis]) for axis in range(len(shape))]
    entries = entries.at[tuple(index_at)].set(smallest)
    longest = shape.index(max(shape))
    index_at[longest] = (index_at[longest] + 1) % shape[longest]
    return entries.at[tuple(index_at)].set(high)


def spiked(drawn, stream_key, source, target, blocks, factor):
    owner, partner = [(jnp.arange(drawn.shape[dim]) // (drawn.shape[dim] // blocks)).reshape([-1 if axis == dim else 1 for axis in range(drawn.ndim)]) for dim in (source, target)]
    chosen = jax.random.permutation(stream_key, blocks)[partner]
    strong = (owner == chosen) | (owner == (partner + blocks // 2) % blocks)
    return jnp.where(strong, factor * drawn, drawn)


def block_scale(rng, extent, shards, least, high):
    def one(dim, blocks):
        draws = jax.random.uniform(jax.random.fold_in(jax.random.fold_in(rng, 6), dim), (blocks,), jnp.float32, least / len(shards), high / len(shards))
        return jnp.repeat(jnp.exp(draws), extent[dim] // blocks).reshape((-1,) + (1,) * (len(extent) - dim - 1))

    loudness = one(*shards[0])
    for cut in shards[1:]:
        loudness = loudness * one(*cut)
    return loudness


def noise(stream_key, shape, deviation, most, shards=(), held_as=jnp.bfloat16):
    array = jax.random.normal(stream_key, shape, jnp.float32) * deviation
    if len(shards) > 0:
        array = block_scale(stream_key, shape, shards, -0.22, 0.18) * array
    return jnp.clip(array, min=-most, max=most).astype(held_as)


def noise_with(rng, dims, deviation, limit, shards, heavy, kind=jnp.bfloat16):
    result = deviation * jax.random.normal(rng, dims, jnp.float32)
    if shards:
        result = result * block_scale(rng, dims, shards, -0.22, 0.18)
    return jnp.clip(spiked(result, jax.random.fold_in(rng, 3), *heavy), -limit, limit).astype(kind)


def setup_inputs(seed: int = 0) -> dict:
    streams_of = jax.random.split(jax.random.key(seed), 12)
    edge_feats = noise_with(streams_of[0], (EDGES, D), 1.0, 6.0, ((0, 32),), (0, 1, 32, 2.75))
    cotangent = noise(streams_of[1], (EDGES, D), 1.0, 6.0, ((0, 32),))
    angle_basis = noise(streams_of[2], (NCBF, TRIPS), 1.0, 6.0, ((1, 32),))
    source_edge = set_ends(jax.random.randint(streams_of[3], (TRIPS,), 0, E_GRP), jax.random.fold_in(streams_of[3], 1), 0, E_GRP - 1).astype(jnp.int32)
    target_edge = set_ends(jax.random.randint(streams_of[4], (TRIPS,), 0, E_DEV), jax.random.fold_in(streams_of[4], 1), 0, E_DEV - 1).astype(jnp.int32)
    pair_weight = noise(streams_of[5], (D, D), D ** -0.5, 0.25, ((0, 8),))
    down_weight = noise(streams_of[6], (D, DT), D ** -0.5, 0.25, ((0, 8),))
    basis_weight = noise(streams_of[7], (NCBF, DT), NCBF ** -0.5, 1.5, ((0, 8),))
    up_weight = noise(streams_of[8], (DT, D), DT ** -0.5, 0.75, ((0, 8),))
    res_first = noise(streams_of[9], (D, D), D ** -0.5, 0.25, ((0, 8),))
    res_second = noise(streams_of[10], (D, D), D ** -0.5, 0.25, ((0, 8),))
    return {"edge_feats": edge_feats, "cotangent": cotangent, "angle_basis": angle_basis, "source_edge": source_edge, "target_edge": target_edge, "pair_weight": pair_weight, "down_weight": down_weight, "basis_weight": basis_weight, "up_weight": up_weight, "res_first": res_first, "res_second": res_second}


def silu_slope(value):
    sig = jax.nn.sigmoid(value)
    return sig * (1.0 + value * (1.0 - sig))

def group_pass(feats, cotan, basis, source, target, pair_weight, down_weight, basis_weight, up_weight, res_first, res_second):
    f32 = jnp.float32
    bf16 = jnp.bfloat16
    scale = math.sqrt(0.5)
    offset = jnp.arange(T_GRP, dtype=jnp.int32) // T_DEV * E_DEV
    outgoing = target + offset
    z_one = jnp.dot(feats, pair_weight, preferred_element_type=f32)
    hidden = jax.nn.silu(z_one).astype(bf16)
    down_t = jnp.einsum('ed,dk->ke', hidden.astype(f32), down_weight.astype(f32)).astype(bf16)
    coeff = jnp.einsum('nk,nt->kt', basis_weight.astype(f32), basis.astype(f32))
    down_in = down_t[:, source].astype(f32)
    agg_t = jnp.zeros((DT, E_GRP), f32).at[:, outgoing].add(down_in * coeff).astype(bf16)
    z_two = jnp.einsum('ke,kd->ed', agg_t.astype(f32), up_weight.astype(f32))
    mixed = jax.nn.silu(z_two).astype(bf16)
    z_three = jnp.dot(mixed, res_first, preferred_element_type=f32)
    inner = jax.nn.silu(z_three).astype(bf16)
    z_four = jnp.dot(inner, res_second, preferred_element_type=f32)
    dz_four = (scale * cotan.astype(f32) * silu_slope(z_four)).astype(bf16)
    second_grad = jnp.dot(inner.T, dz_four, preferred_element_type=f32)
    dz_three = (jnp.dot(dz_four, res_second.T, preferred_element_type=f32) * silu_slope(z_three)).astype(bf16)
    first_grad = jnp.dot(mixed.T, dz_three, preferred_element_type=f32)
    dmixed = scale * cotan.astype(f32) + jnp.dot(dz_three, res_first.T, preferred_element_type=f32)
    dz_two = (dmixed * silu_slope(z_two)).astype(bf16)
    up_grad = jnp.einsum('ke,ed->kd', agg_t.astype(f32), dz_two.astype(f32))
    dagg_t = jnp.einsum('kd,ed->ke', up_weight.astype(f32), dz_two.astype(f32))
    dagg_out = dagg_t[:, outgoing]
    dcoeff = (dagg_out * down_in).astype(bf16)
    basis_grad = jnp.einsum('nt,kt->nk', basis.astype(f32), dcoeff.astype(f32))
    ddown_t = jnp.zeros((DT, E_GRP), f32).at[:, source].add(dagg_out * coeff).astype(bf16)
    down_grad = jnp.einsum('ed,ke->dk', hidden.astype(f32), ddown_t.astype(f32))
    dz_one = (jnp.einsum('ke,dk->ed', ddown_t.astype(f32), down_weight.astype(f32)) * silu_slope(z_one)).astype(bf16)
    pair_grad = jnp.dot(feats.T, dz_one, preferred_element_type=f32)
    edge_grad = jnp.dot(dz_one, pair_weight.T, preferred_element_type=f32).astype(bf16)
    return (edge_grad, (pair_grad, down_grad, basis_grad, up_grad, first_grad, second_grad))

def reference(edge_feats, cotangent, angle_basis, source_edge, target_edge, pair_weight, down_weight, basis_weight, up_weight, res_first, res_second):
    feats = edge_feats.reshape(N_DP, E_GRP, D)
    cotans = cotangent.reshape(N_DP, E_GRP, D)
    bases = jnp.transpose(angle_basis.reshape(NCBF, N_DP, T_GRP), (1, 0, 2))
    sources = source_edge.reshape(N_DP, T_GRP)
    targets = target_edge.reshape(N_DP, T_GRP)
    weights = (pair_weight, down_weight, basis_weight, up_weight, res_first, res_second)
    start = tuple((jnp.zeros(w.shape, jnp.float32) for w in weights))

    def step(carry, items):
        grads, parts = group_pass(items[0], items[1], items[2], items[3], items[4], *weights)
        summed = tuple((c + p for c, p in zip(carry, parts)))
        return (summed, grads)
    totals, grads = lax.scan(step, start, (feats, cotans, bases, sources, targets))
    edge_grad = grads.reshape(EDGES, D)
    return (edge_grad, totals[0], totals[1], totals[2], totals[3], totals[4], totals[5])
```

```python
import functools
import math

import jax
import jax.numpy as jnp
from jax import lax
from jax.experimental import pallas as pl
from jax.experimental.pallas import tpu as pltpu
from jax.sharding import PartitionSpec as P

MESH = pl.DeviceIdType.MESH
F32 = jnp.float32
BF16 = jnp.bfloat16
VM = pl.BlockSpec(memory_space=pltpu.VMEM)
SUB = 256
TILE = 1024
ROWS = 512


def remote(src, dst, send, recv, target):
    return pltpu.make_async_remote_copy(
        src_ref=src,
        dst_ref=dst,
        send_sem=send,
        recv_sem=recv,
        device_id=target,
        device_id_type=MESH,
    )


def sigmoid(value):
    return 0.5 * jnp.tanh(0.5 * value) + 0.5


def slope_of(value, sig):
    return sig * (1.0 + value * (1.0 - sig))


def greet(targets, waits):
    barrier = pltpu.get_barrier_semaphore()
    for target in targets:
        pl.semaphore_signal(barrier, inc=1, device_id=target, device_id_type=MESH)
    pl.semaphore_wait(barrier, waits)


def graph_peers(groups):
    me = lax.axis_index("graph")
    return [{"graph": (me + k) % groups} for k in range(1, groups)]


def chip_peers(n):
    half = n // 2
    dp = lax.axis_index("dp")
    return [{"dp": (dp // 2 + k) % half * 2 + dp % 2} for k in range(1, half)]


def core_peer():
    dp = lax.axis_index("dp")
    return [{"dp": dp + 1 - 2 * (dp % 2)}]


def total_steps(n, groups, kinds, ins, outs, refs):
    count = len(kinds)
    scratch = []
    place_at = 0
    for large in kinds:
        size = 6 if large else 4
        scratch.append(refs[place_at : place_at + size])
        place_at += size
    a_send, a_recv, b_send, b_recv, c_send, c_recv, d_send, d_recv = refs[place_at:]
    half = n // 2
    dp = lax.axis_index("dp")
    me = lax.axis_index("graph")
    pos = dp // 2
    core = dp % 2
    partner = dp + 1 - 2 * core
    sent = []

    def send_all(copies):
        for cp in copies:
            cp.start()
        sent.extend(copies)
        return copies

    first = []
    for w in range(count):
        first.append(
            send_all(
                [
                    remote(
                        ins[w].at[2 * q + 1 - core],
                        scratch[w][0].at[q],
                        a_send.at[w, q],
                        a_recv.at[w, q],
                        {"dp": partner},
                    )
                    for q in range(half)
                ]
            )
        )
    yield
    second = []
    for w, large in enumerate(kinds):
        got, summed = scratch[w][0], scratch[w][1]
        for q in range(half):
            first[w][q].wait_recv()
            value = ins[w][2 * q + core].astype(F32) + got[q].astype(F32)
            if large:
                summed[:, q] = value.astype(summed.dtype)
            else:
                summed[q] = value.astype(summed.dtype)
        copies = []
        if large:
            copies = [
                remote(
                    summed.at[(me + k) % groups],
                    scratch[w][4].at[k],
                    b_send.at[w, k],
                    b_recv.at[w, k],
                    {"graph": (me + k) % groups},
                )
                for k in range(1, groups)
            ]
        second.append(send_all(copies))
    yield
    third = []
    for w, large in enumerate(kinds):
        part = scratch[w][1]
        if large:
            for cp in second[w]:
                cp.wait_recv()
            value = scratch[w][1][me].astype(F32)
            for k in range(1, groups):
                value = value + scratch[w][4][k].astype(F32)
            part = scratch[w][5]
            part[...] = value.astype(part.dtype)
        third.append(
            send_all(
                [
                    remote(
                        part.at[(pos + k) % half],
                        scratch[w][2].at[k],
                        c_send.at[w, k],
                        c_recv.at[w, k],
                        {"dp": (pos + k) % half * 2 + core},
                    )
                    for k in range(1, half)
                ]
            )
        )
    yield
    fourth = []
    for w, large in enumerate(kinds):
        part = scratch[w][5] if large else scratch[w][1]
        for cp in third[w]:
            cp.wait_recv()
        value = part[pos].astype(F32)
        for k in range(1, half):
            value = value + scratch[w][2][k].astype(F32)
        done = scratch[w][3]
        done[...] = value.astype(done.dtype)
        fourth.append(
            send_all(
                [
                    remote(
                        done,
                        outs[w].at[me],
                        d_send.at[w, k],
                        d_recv.at[w, k],
                        {"graph": (me + k) % groups},
                    )
                    for k in range(1, groups)
                ]
            )
        )
        outs[w][me] = value.astype(done.dtype)
    yield
    for copies in fourth:
        for cp in copies:
            cp.wait_recv()
    for cp in sent:
        cp.wait_send()


def total_parts(n, groups, grads, kinds):
    half = n // 2
    shapes, scratch = [], []
    for item, large in zip(grads, kinds):
        tail = item.shape[2:] if large else item.shape[1:]
        kind = item.dtype
        shapes.append(jax.ShapeDtypeStruct((groups,) + tail, kind))
        scratch.append(pltpu.VMEM((half,) + item.shape[1:], kind))
        scratch.append(
            pltpu.VMEM(((groups, half) + tail) if large else ((half,) + tail), kind)
        )
        scratch.append(pltpu.VMEM((half,) + tail, kind))
        scratch.append(pltpu.VMEM(tail, kind))
        if large:
            scratch.append(pltpu.VMEM((groups, half) + tail, kind))
            scratch.append(pltpu.VMEM((half,) + tail, kind))
    for length in (half, groups, half, groups):
        scratch += [pltpu.SemaphoreType.DMA((len(grads), length))] * 2
    return shapes, scratch


def greet_all(n, groups):
    greet(core_peer() + graph_peers(groups) + chip_peers(n), groups + n // 2 - 1)


def one_hot(size, row):
    spots = lax.broadcasted_iota(jnp.int32, (size, row.shape[1]), 0)
    return jnp.where(spots == row, 1.0, 0.0).astype(BF16)


def pick(stack, owner, groups, width):
    value = jnp.where(owner == 0, stack[:width], 0.0)
    for g in range(1, groups):
        value = value + jnp.where(owner == g, stack[g * width : (g + 1) * width], 0.0)
    return value


def place(value, owner, groups):
    return jnp.concatenate(
        [jnp.where(owner == g, value, 0.0).astype(BF16) for g in range(groups)], axis=0
    )


def dot(a, b, dims):
    return lax.dot_general(a, b, (dims, ((), ())), preferred_element_type=F32)


NN = ((1,), (0,))
NT = ((1,), (1,))
TN = ((0,), (0,))


class Gather:
    def __init__(self, n, ins, outs, send, recv):
        self.ins, self.outs, self.send, self.recv = ins, outs, send, recv
        self.count = len(ins)
        self.half = n // 2
        self.dp = lax.axis_index("dp")
        self.pos = self.dp // 2
        self.core = self.dp % 2
        self.partner = self.dp + 1 - 2 * self.core
        self.has_up = self.pos < self.half - 1
        self.has_down = self.pos > 0

    def copy(self, w, src, shard, way, target):
        return remote(
            src,
            self.outs[w].at[shard],
            self.send.at[shard, way, w],
            self.recv.at[shard, w],
            {"dp": target},
        )

    def pass_on(self, w, src, shard, way):
        target = (self.dp + 2, self.dp - 2, self.partner)[way]
        self.copy(w, src, shard, way, target).start()

    def start(self):
        for w in range(self.count):
            src = self.ins[w]

            @pl.when(self.has_up)
            def _():
                self.pass_on(w, src, self.dp, 0)

            @pl.when(self.has_down)
            def _():
                self.pass_on(w, src, self.dp, 1)

            self.pass_on(w, src, self.dp, 2)
        for w in range(self.count):
            self.outs[w][self.dp] = self.ins[w][...]

    def arrive(self, w, shard):
        self.copy(w, self.outs[w].at[shard], shard, 2, self.partner).wait_recv()

    def hop(self, k):
        for w in range(self.count):

            @pl.when(self.pos >= k)
            def _():
                shard = self.dp - 2 * k
                self.arrive(w, shard)

                @pl.when(self.has_up)
                def _():
                    self.pass_on(w, self.outs[w].at[shard], shard, 0)

                self.pass_on(w, self.outs[w].at[shard], shard, 2)

            @pl.when(self.pos + k < self.half)
            def _():
                shard = self.dp + 2 * k
                self.arrive(w, shard)

                @pl.when(self.has_down)
                def _():
                    self.pass_on(w, self.outs[w].at[shard], shard, 1)

                self.pass_on(w, self.outs[w].at[shard], shard, 2)

    def across(self, k):
        for w in range(self.count):
            if k == 0:
                self.arrive(w, self.partner)
                continue

            @pl.when(self.pos >= k)
            def _():
                self.arrive(w, self.partner - 2 * k)

            @pl.when(self.pos + k < self.half)
            def _():
                self.arrive(w, self.partner + 2 * k)

    def drain(self):
        for w in range(self.count):
            for q in range(self.half):
                mine = 2 * q + self.core
                block = self.outs[w].at[mine]
                self.copy(w, block, mine, 2, self.partner).wait_send()

                @pl.when(jnp.logical_and(self.pos >= q, self.has_up))
                def _():
                    self.copy(w, block, mine, 0, self.dp + 2).wait_send()

                @pl.when(jnp.logical_and(self.pos <= q, self.has_down))
                def _():
                    self.copy(w, block, mine, 1, self.dp - 2).wait_send()


def whole(ref):
    value = ref[...]
    return value.reshape(-1, value.shape[2])


def spread(ref, value, col=0):
    value = value.astype(ref.dtype)
    lead = ref.shape[:-2]
    rows = ref.shape[-2]
    for i in range(math.prod(lead)):
        part = value[i * rows : (i + 1) * rows]
        if len(lead) == 2:
            ref[i // lead[1], i % lead[1]] = part
        else:
            ref[i] = part


def by_tile(total, tile, body):
    def step(i, carry):
        body(pl.ds(pl.multiple_of(i * tile, tile), tile))
        return carry

    lax.fori_loop(0, total // tile, step, 0)


def block_kernel(n, groups, names, plans, *refs):
    r = dict(zip(names, refs))
    feats, cot, basis = r["feats"], r["cot"], r["basis"]
    src_ref, tgt_ref = r["src"], r["tgt"]
    z_one, hidden, table, acc = r["z_one"], r["hidden"], r["table"], r["acc"]
    edges, dim = feats.shape
    width = r["down"].shape[1]
    trips = src_ref.shape[1]
    subs = edges // SUB
    half = n // 2
    scale = math.sqrt(0.5)
    me = lax.axis_index("graph")
    tile = min(TILE, trips)
    tiles = trips // tile

    def sems(name):
        return r[name + "_send"], r[name + "_recv"]

    def total(name):
        kinds, count = plans[name]
        return total_steps(
            n,
            groups,
            kinds,
            [r[f"{name}_in{w}"] for w in range(len(kinds))],
            [r[f"{name}_out{w}"] for w in range(len(kinds))],
            [r[f"{name}_s{i}"] for i in range(count)],
        )

    greet_all(n, groups)
    early = Gather(
        n,
        (r["pair"], r["down"], r["wb"]),
        (r["w_pair"], r["w_down"], r["w_basis"]),
        *sems("early"),
    )
    late = Gather(
        n,
        (r["up"], r["first"], r["second"]),
        (r["w_up"], r["w_first"], r["w_second"]),
        *sems("late"),
    )
    early.start()
    w_pair = r["w_pair"]
    depth = 2 * w_pair.shape[1]
    split = depth % 128 == 0

    def meet(chip, fresh=False):
        weight = w_pair[pl.ds(2 * chip, 2)].reshape(depth, dim)
        cols = pl.ds(pl.multiple_of(chip * depth, depth), depth)

        def body(rows):
            value = dot(feats[rows, cols], weight, NN)
            z_one[rows, :] = value if fresh else z_one[rows, :] + value

        by_tile(edges, 256, body)

    early.across(0)
    if split:
        meet(early.pos, True)
    for k in range(1, half):
        early.hop(k)
        early.across(k)
        if split:

            @pl.when(early.pos >= k)
            def _():
                meet(early.pos - k)

            @pl.when(early.pos + k < half)
            def _():
                meet(early.pos + k)

    late.start()
    if not split:

        def body(rows):
            z_one[rows, :] = dot(feats[rows, :], whole(w_pair), NN)

        by_tile(edges, 256, body)

    down_own = r["down_own"]
    f_send, f_recv = sems("fwd")
    ahead = []
    for c in range(subs):
        rows = slice(c * SUB, (c + 1) * SUB)
        value = z_one[rows, :]
        sig = sigmoid(value)
        act = (value * sig).astype(BF16)
        hidden[rows, :] = act
        down_own[c] = dot(whole(r["w_down"]), act, ((0,), (1,))).astype(BF16)
        table[me, :, rows] = down_own[c]
        for k in range(1, groups):
            cp = remote(
                down_own.at[c],
                table.at[me, :, rows],
                f_send.at[k, c],
                f_recv.at[k, c],
                {"graph": (me + k) % groups},
            )
            cp.start()
            ahead.append(cp)
        z_one[rows, :] = slope_of(value, sig)
    late.across(0)
    late.hop(1)
    acc[...] = jnp.zeros_like(acc)
    w_basis = whole(r["w_basis"])
    din = r["din"]

    def gather_tile(i, carry):
        spot = pl.ds(pl.multiple_of(i * tile, tile), tile)
        src = src_ref[:, spot]
        tgt = tgt_ref[:, spot]
        owner = src // edges
        stack = dot(
            table[...].reshape(groups * width, edges), one_hot(edges, src - owner * edges), NN
        )
        down_in = pick(stack, owner, groups, width)
        din[:, spot] = down_in.astype(BF16)
        coeff = dot(w_basis, basis[:, spot], TN)
        high = tgt // SUB
        acc[...] += dot(
            place(down_in * coeff, high, subs), one_hot(SUB, tgt - high * SUB), NT
        )
        return carry

    for cp in ahead:
        cp.wait()
    hops = list(range(2, half))
    for i in range(len(hops) + 1):
        low = tiles * i // (len(hops) + 1)
        high = tiles * (i + 1) // (len(hops) + 1)
        lax.fori_loop(low, high, gather_tile, 0)
        if i < len(hops):
            late.hop(hops[i])
    agg = r["agg"]
    for h in range(subs):
        agg[:, h * SUB : (h + 1) * SUB] = acc[h * width : (h + 1) * width, :].astype(BF16)
    for k in range(1, half):
        late.across(k)

    mixed, inner = r["mixed"], r["inner"]
    slope_two, slope_three = r["slope_two"], r["slope_three"]
    dz_four, dz_three, dz_two = r["dz_four"], r["dz_three"], r["dz_two"]
    block = min(ROWS, edges)

    def outward(rows):
        value = dot(agg[:, rows], whole(r["w_up"]), TN)
        sig = sigmoid(value)
        act = (value * sig).astype(BF16)
        mixed[rows, :] = act
        slope_two[rows, :] = slope_of(value, sig)
        value = dot(act, whole(r["w_first"]), NN)
        sig = sigmoid(value)
        act = (value * sig).astype(BF16)
        inner[rows, :] = act
        slope_three[rows, :] = slope_of(value, sig)
        value = dot(act, whole(r["w_second"]), NN)
        slope = slope_of(value, sigmoid(value))
        dz_four[rows, :] = (scale * cot[rows, :].astype(F32) * slope).astype(BF16)

    by_tile(edges, block, outward)
    spread(r["second_in0"], dot(inner[...], dz_four[...], TN))
    second = total("second")
    next(second)

    def inward(rows):
        value = dot(dz_four[rows, :], whole(r["w_second"]), NT) * slope_three[rows, :]
        dz_three[rows, :] = value.astype(BF16)

    by_tile(edges, block, inward)
    next(second)
    spread(r["first_in0"], dot(mixed[...], dz_three[...], TN))
    first = total("first")
    next(first)
    dagg = r["dagg"]

    def through(rows):
        value = scale * cot[rows, :].astype(F32) + dot(
            dz_three[rows, :], whole(r["w_first"]), NT
        )
        value = (value * slope_two[rows, :]).astype(BF16)
        dz_two[rows, :] = value

    by_tile(edges, block, through)
    next(first)
    for h in range(subs):
        rows = slice(h * SUB, (h + 1) * SUB)
        dagg[h * width : (h + 1) * width, :] = dot(
            whole(r["w_up"]), dz_two[rows, :], NT
        ).astype(BF16)
    spread(r["up_in0"], dot(agg[...], dz_two[...], NN))
    up = total("up")
    next(up)

    placed, basis_sum = r["placed"], r["basis_sum"]
    basis_sum[...] = jnp.zeros_like(basis_sum)

    def spread_tile(spot):
        src = src_ref[:, spot]
        tgt = tgt_ref[:, spot]
        owner = src // edges
        high = tgt // SUB
        dagg_out = pick(dot(dagg[...], one_hot(SUB, tgt - high * SUB), NN), high, subs, width)
        dcoeff = (dagg_out * din[:, spot].astype(F32)).astype(BF16)
        basis_sum[...] += dot(basis[:, spot], dcoeff, NT)
        coeff = dot(w_basis, basis[:, spot], TN)
        placed[:, spot] = place(dagg_out * coeff, owner, groups)

    by_tile(trips, tile, spread_tile)
    next(second)
    next(up)
    basis_plan = total("basis")
    spread(r["basis_in0"], basis_sum[...])
    next(basis_plan)
    parts, landed = r["parts"], r["landed"]
    b_send, b_recv = sems("bwd")
    back = []
    chunk_sum = r["chunk_sum"]
    calls = {0: (first, second), 1: (up, basis_plan), 2: (first,), 3: ()}
    for c in range(subs):
        chunk_sum[...] = jnp.zeros_like(chunk_sum)

        def scatter_tile(spot):
            src = src_ref[:, spot]
            spots = src - src // edges * edges - c * SUB
            chunk_sum[...] += dot(placed[:, spot], one_hot(SUB, spots), NT)

        by_tile(trips, tile, scatter_tile)
        for g in range(groups):
            parts[g, c] = chunk_sum[g * width : (g + 1) * width, :].astype(BF16)
        for k in range(1, groups):
            peer = (me + k) % groups
            cp = remote(
                parts.at[peer, c], landed.at[k, c], b_send.at[k, c], b_recv.at[k, c], {"graph": peer}
            )
            cp.start()
            back.append(cp)
        for steps in calls.get(c, ()):
            next(steps)
    for steps in (up, basis_plan):
        next(steps)
    for cp in back:
        cp.wait()

    ddown, dz_one = r["ddown"], r["dz_one"]
    for c in range(subs):
        value = parts[me, c].astype(F32)
        for k in range(1, groups):
            value = value + landed[k, c].astype(F32)
        value = value.astype(BF16)
        rows = slice(c * SUB, (c + 1) * SUB)
        ddown[:, rows] = value
        slope = z_one[rows, :]
        dz_one[rows, :] = (dot(value, whole(r["w_down"]), ((0,), (1,))) * slope).astype(BF16)
    cols = dim // 2
    spread(r["pair_a_in0"], dot(feats[...], dz_one[:, :cols], TN))
    pair_a = total("pair_a")
    next(pair_a)
    spread(r["pair_b_in0"], dot(feats[...], dz_one[:, cols:], TN))
    pair_b = total("pair_b")
    next(pair_b)
    next(pair_a)
    spread(r["down_grad_in0"], dot(hidden[...], ddown[...], ((0,), (1,))))
    down_plan = total("down_grad")
    next(down_plan)
    next(pair_b)
    edge = r["edge"]

    def input_grad(rows):
        edge[rows, :] = dot(dz_one[rows, :], whole(w_pair), NT).astype(BF16)

    by_tile(edges // 2, block // 2, input_grad)
    next(pair_a)
    next(down_plan)
    next(pair_b)
    by_tile(edges // 2, block // 2, lambda rows: input_grad(pl.ds(rows.start + edges // 2, rows.size)))
    next(pair_a)
    next(down_plan)
    next(pair_b)
    next(down_plan)
    for steps in (second, first, up, basis_plan, pair_a, pair_b, down_plan):
        for _ in steps:
            pass
    for gather in (early, late):
        gather.drain()


def on_device(
    edge_feats,
    cotangent,
    angle_basis,
    source_edge,
    target_edge,
    pair_weight,
    down_weight,
    basis_weight,
    up_weight,
    res_first,
    res_second,
):
    n = lax.axis_size("dp")
    groups = lax.axis_size("graph")
    edges, dim = edge_feats.shape
    width = down_weight.shape[1]
    trips = source_edge.shape[0]
    subs = edges // SUB
    names, shapes = [], []

    def hold(name, *shape, kind=BF16):
        names.append(name)
        shapes.append(pltpu.VMEM(shape, kind))

    def flags(name, *shape):
        names.extend((name + "_send", name + "_recv"))
        shapes.extend([pltpu.SemaphoreType.DMA(shape)] * 2)

    args = dict(
        feats=edge_feats,
        cot=cotangent,
        basis=angle_basis,
        src=source_edge.reshape(1, -1),
        tgt=target_edge.reshape(1, -1),
        pair=pair_weight,
        down=down_weight,
        wb=basis_weight,
        up=up_weight,
        first=res_first,
        second=res_second,
    )
    outs = {"edge": jax.ShapeDtypeStruct((edges, dim), BF16)}
    plans = {}

    def plan(name, rows, cols, large, kind=BF16):
        shape = (n, groups, rows // (n * groups), cols) if large else (n, rows // n, cols)
        item = jax.ShapeDtypeStruct(shape, kind)
        landing, scratch = total_parts(n, groups, (item,), (large,))
        outs[name + "_out0"] = landing[0]
        hold(name + "_in0", *shape, kind=kind)
        for i, extra in enumerate(scratch):
            names.append(f"{name}_s{i}")
            shapes.append(extra)
        plans[name] = ((large,), len(scratch))

    plan("pair_a", dim, dim // 2, True)
    plan("pair_b", dim, dim // 2, True)
    plan("down_grad", dim, width, False)
    plan("basis", angle_basis.shape[0], width, False, F32)
    plan("up", width, dim, False)
    plan("first", dim, dim, True)
    plan("second", dim, dim, True)
    for name, shard in (
        ("w_pair", pair_weight),
        ("w_down", down_weight),
        ("w_basis", basis_weight),
        ("w_up", up_weight),
        ("w_first", res_first),
        ("w_second", res_second),
    ):
        hold(name, n, *shard.shape)
    for name in ("z_one", "slope_two", "slope_three"):
        hold(name, edges, dim, kind=F32)
    for name in ("hidden", "mixed", "inner", "dz_four", "dz_three", "dz_two", "dz_one"):
        hold(name, edges, dim)
    hold("table", groups, width, edges)
    hold("down_own", subs, width, SUB)
    hold("acc", subs * width, SUB, kind=F32)
    hold("din", width, trips)
    hold("agg", width, edges)
    hold("dagg", subs * width, SUB)
    hold("placed", groups * width, trips)
    hold("basis_sum", angle_basis.shape[0], width, kind=F32)
    hold("chunk_sum", groups * width, SUB, kind=F32)
    hold("parts", groups, subs, width, SUB)
    hold("landed", groups, subs, width, SUB)
    hold("ddown", width, edges)
    flags("early", n, 3, 3)
    names[-1:], shapes[-1:] = ["early_recv"], [pltpu.SemaphoreType.DMA((n, 3))]
    flags("late", n, 3, 3)
    names[-1:], shapes[-1:] = ["late_recv"], [pltpu.SemaphoreType.DMA((n, 3))]
    flags("fwd", groups, subs)
    flags("bwd", groups, subs)
    results = pl.pallas_call(
        functools.partial(block_kernel, n, groups, list(args) + list(outs) + names, plans),
        out_shape=list(outs.values()),
        in_specs=[VM] * len(args),
        out_specs=[VM] * len(outs),
        scratch_shapes=shapes,
        compiler_params=pltpu.CompilerParams(collective_id=0, has_side_effects=True),
        name="block",
    )(*args.values())
    got = dict(zip(outs, results))
    return write_grads(got, groups)


def write_kernel(ins, outs, *refs):
    landed = dict(zip(ins, refs))
    for name, out in zip(outs, refs[len(ins) :]):
        if name == "edge":
            out[...] = landed["edge"][...]
            continue
        col = 0
        for part in (name,) if name in landed else (name + "_a", name + "_b"):
            item = landed[part]
            groups, rows, cols = item.shape
            spot = slice(col, col + cols)
            col += cols
            if name in SHARED:
                value = item[0].astype(F32)
                for g in range(1, groups):
                    value = value + item[g].astype(F32)
                out[:, spot] = value
            else:
                for g in range(groups):
                    out[g * rows : (g + 1) * rows, spot] = item[g].astype(F32)


SHARED = ("down_grad", "basis", "up")


def write_grads(got, groups):
    got = {name.removesuffix("_out0"): item for name, item in got.items()}
    dim = got["edge"].shape[1]
    outs = {"edge": jax.ShapeDtypeStruct(got["edge"].shape, BF16)}
    for name in ("pair", "down_grad", "basis", "up", "first", "second"):
        item = got[name] if name in got else got[name + "_a"]
        rows = item.shape[1] * (1 if name in SHARED else groups)
        cols = item.shape[2] if name in got else dim
        outs[name] = jax.ShapeDtypeStruct((rows, cols), F32)
    return tuple(
        pl.pallas_call(
            functools.partial(write_kernel, list(got), list(outs)),
            out_shape=list(outs.values()),
            in_specs=[VM] * len(got),
            out_specs=[VM] * len(outs),
            name="write_grads",
        )(*got.values())
    )


def solution(mesh):
    return jax.shard_map(
        on_device,
        mesh=mesh,
        in_specs=(
            P(("dp", "graph"), None),
            P(("dp", "graph"), None),
            P(None, ("dp", "graph")),
            P(("dp", "graph")),
            P(("dp", "graph")),
            P("dp", None),
            P("dp", None),
            P("dp", None),
            P("dp", None),
            P("dp", None),
            P("dp", None),
        ),
        out_specs=(
            P(("dp", "graph"), None),
            P("dp", None),
            P("dp", None),
            P("dp", None),
            P("dp", None),
            P("dp", None),
            P("dp", None),
        ),
        check_vma=False,
    )
```

```python
import functools
import math

import jax
import jax.numpy as jnp
from jax import lax
from jax.experimental import pallas as pl
from jax.experimental.pallas import tpu as pltpu
from jax.sharding import PartitionSpec as P

MESH = pl.DeviceIdType.MESH
F32 = jnp.float32
BF16 = jnp.bfloat16
VM = pl.BlockSpec(memory_space=pltpu.VMEM)
ANY = pl.BlockSpec(memory_space=pl.ANY)
SUB = 256
TILE = 2048
SPAN = 2048
PASSES = 2
LOADED = ("feats", "basis", "src", "tgt", "cot")
PIECE = 16
ROWS = 512


def remote(src, dst, send, recv, target):
    return pltpu.make_async_remote_copy(
        src_ref=src,
        dst_ref=dst,
        send_sem=send,
        recv_sem=recv,
        device_id=target,
        device_id_type=MESH,
    )


def sigmoid(value):
    return 0.5 * jnp.tanh(0.5 * value) + 0.5


def slope_of(value, sig):
    return sig * (1.0 + value * (1.0 - sig))


def greet(targets, waits):
    barrier = pltpu.get_barrier_semaphore()
    for target in targets:
        pl.semaphore_signal(barrier, inc=1, device_id=target, device_id_type=MESH)
    pl.semaphore_wait(barrier, waits)


def graph_peers(groups):
    me = lax.axis_index("graph")
    return [{"graph": (me + k) % groups} for k in range(1, groups)]


def chip_peers(n):
    half = n // 2
    dp = lax.axis_index("dp")
    return [{"dp": (dp // 2 + k) % half * 2 + dp % 2} for k in range(1, half)]


def core_peer():
    dp = lax.axis_index("dp")
    return [{"dp": dp + 1 - 2 * (dp % 2)}]


def total_steps(n, groups, kinds, ins, outs, refs):
    count = len(kinds)
    scratch = []
    place_at = 0
    for large in kinds:
        size = 6 if large else 4
        scratch.append(refs[place_at : place_at + size])
        place_at += size
    a_send, a_recv, b_send, b_recv, c_send, c_recv, d_send, d_recv = refs[place_at:]
    half = n // 2
    dp = lax.axis_index("dp")
    me = lax.axis_index("graph")
    pos = dp // 2
    core = dp % 2
    partner = dp + 1 - 2 * core
    sent = []

    def send_all(copies):
        for cp in copies:
            cp.start()
        sent.extend(copies)
        return copies

    first = []
    for w in range(count):
        first.append(
            send_all(
                [
                    remote(
                        ins[w].at[2 * q + 1 - core],
                        scratch[w][0].at[q],
                        a_send.at[w, q],
                        a_recv.at[w, q],
                        {"dp": partner},
                    )
                    for q in range(half)
                ]
            )
        )
    yield
    second = []
    for w, large in enumerate(kinds):
        got, summed = scratch[w][0], scratch[w][1]
        for q in range(half):
            first[w][q].wait_recv()
            value = ins[w][2 * q + core].astype(F32) + got[q].astype(F32)
            if large:
                summed[:, q] = value.astype(summed.dtype)
            else:
                summed[q] = value.astype(summed.dtype)
        copies = []
        if large:
            copies = [
                remote(
                    summed.at[(me + k) % groups],
                    scratch[w][4].at[k],
                    b_send.at[w, k],
                    b_recv.at[w, k],
                    {"graph": (me + k) % groups},
                )
                for k in range(1, groups)
            ]
        second.append(send_all(copies))
    yield
    third = []
    for w, large in enumerate(kinds):
        part = scratch[w][1]
        if large:
            for cp in second[w]:
                cp.wait_recv()
            value = scratch[w][1][me].astype(F32)
            for k in range(1, groups):
                value = value + scratch[w][4][k].astype(F32)
            part = scratch[w][5]
            part[...] = value.astype(part.dtype)
        third.append(
            send_all(
                [
                    remote(
                        part.at[(pos + k) % half],
                        scratch[w][2].at[k],
                        c_send.at[w, k],
                        c_recv.at[w, k],
                        {"dp": (pos + k) % half * 2 + core},
                    )
                    for k in range(1, half)
                ]
            )
        )
    yield
    fourth = []
    for w, large in enumerate(kinds):
        part = scratch[w][5] if large else scratch[w][1]
        for cp in third[w]:
            cp.wait_recv()
        value = part[pos].astype(F32)
        for k in range(1, half):
            value = value + scratch[w][2][k].astype(F32)
        done = scratch[w][3]
        done[...] = value.astype(done.dtype)
        fourth.append(
            send_all(
                [
                    remote(
                        done,
                        outs[w].at[me],
                        d_send.at[w, k],
                        d_recv.at[w, k],
                        {"graph": (me + k) % groups},
                    )
                    for k in range(1, groups)
                ]
            )
        )
        outs[w][me] = value.astype(done.dtype)
    yield
    for copies in fourth:
        for cp in copies:
            cp.wait_recv()
    for cp in sent:
        cp.wait_send()


def total_parts(n, groups, grads, kinds):
    half = n // 2
    shapes, scratch = [], []
    for item, large in zip(grads, kinds):
        tail = item.shape[2:] if large else item.shape[1:]
        kind = item.dtype
        shapes.append(jax.ShapeDtypeStruct((groups,) + tail, kind))
        scratch.append(pltpu.VMEM((half,) + item.shape[1:], kind))
        scratch.append(
            pltpu.VMEM(((groups, half) + tail) if large else ((half,) + tail), kind)
        )
        scratch.append(pltpu.VMEM((half,) + tail, kind))
        scratch.append(pltpu.VMEM(tail, kind))
        if large:
            scratch.append(pltpu.VMEM((groups, half) + tail, kind))
            scratch.append(pltpu.VMEM((half,) + tail, kind))
    for length in (half, groups, half, groups):
        scratch += [pltpu.SemaphoreType.DMA((len(grads), length))] * 2
    return shapes, scratch


def greet_all(n, groups):
    greet(core_peer() + graph_peers(groups) + chip_peers(n), groups + n // 2 - 1)


def one_hot(size, row):
    spots = lax.broadcasted_iota(jnp.int32, (size, row.shape[1]), 0)
    return jnp.where(spots == row, 1.0, 0.0).astype(BF16)


def pick(stack, owner, groups, width):
    value = jnp.where(owner == 0, stack[:width], 0.0)
    for g in range(1, groups):
        value = value + jnp.where(owner == g, stack[g * width : (g + 1) * width], 0.0)
    return value


def place(value, owner, groups):
    return jnp.concatenate(
        [jnp.where(owner == g, value, 0.0).astype(BF16) for g in range(groups)], axis=0
    )


def dot(a, b, dims):
    return lax.dot_general(a, b, (dims, ((), ())), preferred_element_type=F32)


NN = ((1,), (0,))
NT = ((1,), (1,))
TN = ((0,), (0,))


class Gather:
    def __init__(self, n, ins, outs, send, recv):
        self.ins, self.outs, self.send, self.recv = ins, outs, send, recv
        self.count = len(ins)
        self.half = n // 2
        self.dp = lax.axis_index("dp")
        self.pos = self.dp // 2
        self.core = self.dp % 2
        self.partner = self.dp + 1 - 2 * self.core
        self.has_up = self.pos < self.half - 1
        self.has_down = self.pos > 0

    def copy(self, w, src, shard, way, target):
        return remote(
            src,
            self.outs[w].at[shard],
            self.send.at[shard, way, w],
            self.recv.at[shard, w],
            {"dp": target},
        )

    def pass_on(self, w, src, shard, way):
        target = (self.dp + 2, self.dp - 2, self.partner)[way]
        self.copy(w, src, shard, way, target).start()

    def start(self):
        for w in range(self.count):
            src = self.ins[w]

            @pl.when(self.has_up)
            def _():
                self.pass_on(w, src, self.dp, 0)

            @pl.when(self.has_down)
            def _():
                self.pass_on(w, src, self.dp, 1)

            self.pass_on(w, src, self.dp, 2)
        for w in range(self.count):
            self.outs[w][self.dp] = self.ins[w][...]

    def arrive(self, w, shard):
        self.copy(w, self.outs[w].at[shard], shard, 2, self.partner).wait_recv()

    def hop(self, k):
        for w in range(self.count):

            @pl.when(self.pos >= k)
            def _():
                shard = self.dp - 2 * k
                self.arrive(w, shard)

                @pl.when(self.has_up)
                def _():
                    self.pass_on(w, self.outs[w].at[shard], shard, 0)

                self.pass_on(w, self.outs[w].at[shard], shard, 2)

            @pl.when(self.pos + k < self.half)
            def _():
                shard = self.dp + 2 * k
                self.arrive(w, shard)

                @pl.when(self.has_down)
                def _():
                    self.pass_on(w, self.outs[w].at[shard], shard, 1)

                self.pass_on(w, self.outs[w].at[shard], shard, 2)

    def across(self, k):
        for w in range(self.count):
            if k == 0:
                self.arrive(w, self.partner)
                continue

            @pl.when(self.pos >= k)
            def _():
                self.arrive(w, self.partner - 2 * k)

            @pl.when(self.pos + k < self.half)
            def _():
                self.arrive(w, self.partner + 2 * k)

    def drain(self):
        for w in range(self.count):
            for q in range(self.half):
                mine = 2 * q + self.core
                block = self.outs[w].at[mine]
                self.copy(w, block, mine, 2, self.partner).wait_send()

                @pl.when(jnp.logical_and(self.pos >= q, self.has_up))
                def _():
                    self.copy(w, block, mine, 0, self.dp + 2).wait_send()

                @pl.when(jnp.logical_and(self.pos <= q, self.has_down))
                def _():
                    self.copy(w, block, mine, 1, self.dp - 2).wait_send()


def pieces(rows):
    size = PIECE if rows % PIECE == 0 else rows
    return [pl.ds(i * size, size) for i in range(rows // size)]


def whole(ref):
    value = ref[...]
    return value.reshape(-1, value.shape[2])


def spread(ref, value, col=0):
    value = value.astype(ref.dtype)
    lead = ref.shape[:-2]
    rows = ref.shape[-2]
    for i in range(math.prod(lead)):
        part = value[i * rows : (i + 1) * rows]
        if len(lead) == 2:
            ref[i // lead[1], i % lead[1]] = part
        else:
            ref[i] = part


def by_tile(total, tile, body):
    def step(i, carry):
        body(pl.ds(pl.multiple_of(i * tile, tile), tile))
        return carry

    lax.fori_loop(0, total // tile, step, 0)


def block_kernel(n, groups, names, plans, *refs):
    r = dict(zip(names, refs))
    feats, cot, basis = r["feats"], r["cot"], r["basis"]
    src_ref, tgt_ref = r["src"], r["tgt"]
    z_one, hidden, table, acc = r["z_one"], r["hidden"], r["table"], r["acc"]
    edges, dim = feats.shape
    width = r["down"].shape[1]
    trips = src_ref.shape[1]
    subs = edges // SUB
    half = n // 2
    scale = math.sqrt(0.5)
    me = lax.axis_index("graph")
    tile = min(TILE, trips)
    tiles = trips // tile

    def sems(name):
        return r[name + "_send"], r[name + "_recv"]

    def total(name):
        kinds, count = plans[name]
        return total_steps(
            n,
            groups,
            kinds,
            [r[f"{name}_in{w}"] for w in range(len(kinds))],
            [r[f"{name}_out{w}"] for w in range(len(kinds))],
            [r[f"{name}_s{i}"] for i in range(count)],
        )

    loads = {}
    for i, name in enumerate(LOADED):
        loads[name] = pltpu.make_async_copy(r[name + "_far"], r[name], r["loads"].at[i])
        loads[name].start()
    greet_all(n, groups)
    cuts = pieces(r["pair"].shape[0])
    early = Gather(
        n,
        [r["pair"].at[rows] for rows in cuts] + [r["down"], r["wb"]],
        [r["w_pair"].at[:, rows] for rows in cuts] + [r["w_down"], r["w_basis"]],
        *sems("early"),
    )
    late = Gather(
        n,
        (r["up"], r["first"], r["second"]),
        (r["w_up"], r["w_first"], r["w_second"]),
        *sems("late"),
    )
    early.start()
    w_pair = r["w_pair"]
    for k in range(1, half):
        early.hop(k)
    late.start()
    for k in range(half):
        early.across(k)
    loads["feats"].wait()
    down_own = r["down_own"]
    f_send, f_recv = sems("fwd")
    ahead = []
    for c in range(subs):
        rows = slice(c * SUB, (c + 1) * SUB)
        value = dot(feats[rows, :], whole(w_pair), NN)
        sig = sigmoid(value)
        act = (value * sig).astype(BF16)
        hidden[rows, :] = act
        down_own[c] = dot(whole(r["w_down"]), act, ((0,), (1,))).astype(BF16)
        table[me, :, rows] = down_own[c]
        ahead.append([])
        for k in range(1, groups):
            cp = remote(
                down_own.at[c],
                table.at[me, :, rows],
                f_send.at[k, c],
                f_recv.at[k, c],
                {"graph": (me + k) % groups},
            )
            cp.start()
            ahead[c].append(cp)
        z_one[rows, :] = slope_of(value, sig)
    acc[...] = jnp.zeros_like(acc)
    w_basis = whole(r["w_basis"])
    din = r["din"]
    reach = edges // PASSES
    for name in ("basis", "src", "tgt"):
        loads[name].wait()

    def gather_tile(part, i, carry):
        spot = pl.ds(pl.multiple_of(i * tile, tile), tile)
        src = src_ref[:, spot]
        owner = src // edges
        cols = slice(part * reach, (part + 1) * reach)
        stack = dot(
            table[:, :, cols].reshape(groups * width, reach),
            one_hot(reach, src - owner * edges - part * reach),
            NN,
        )
        down_in = pick(stack, owner, groups, width)
        if part > 0:
            down_in = down_in + din[:, spot].astype(F32)
        din[:, spot] = down_in.astype(BF16)
        if part == PASSES - 1:
            tgt = tgt_ref[:, spot]
            coeff = dot(w_basis, basis[:, spot], TN)
            high = tgt // SUB
            acc[...] += dot(
                place(down_in * coeff, high, subs), one_hot(SUB, tgt - high * SUB), NT
            )
        return carry

    units = PASSES * tiles
    stops = {max(units * k // half - 1, 0): k for k in range(1, half)}
    for part in range(PASSES):
        for c in range(subs * part // PASSES, subs * (part + 1) // PASSES):
            for cp in ahead[c]:
                cp.wait()
        low = 0
        for unit in range(tiles):
            if part * tiles + unit in stops:
                lax.fori_loop(low, unit, functools.partial(gather_tile, part), 0)
                low = unit
                late.hop(stops[part * tiles + unit])
        lax.fori_loop(low, tiles, functools.partial(gather_tile, part), 0)
    late.across(0)
    agg = r["agg"]
    for h in range(subs):
        agg[:, h * SUB : (h + 1) * SUB] = acc[h * width : (h + 1) * width, :].astype(BF16)
    for k in range(1, half):
        late.across(k)

    loads["cot"].wait()
    mixed, inner = r["mixed"], r["inner"]
    slope_two, slope_three = r["slope_two"], r["slope_three"]
    dz_four, dz_three, dz_two = r["dz_four"], r["dz_three"], r["dz_two"]
    block = min(ROWS, edges)

    def outward(rows):
        value = dot(agg[:, rows], whole(r["w_up"]), TN)
        sig = sigmoid(value)
        act = (value * sig).astype(BF16)
        mixed[rows, :] = act
        slope_two[rows, :] = slope_of(value, sig)
        value = dot(act, whole(r["w_first"]), NN)
        sig = sigmoid(value)
        act = (value * sig).astype(BF16)
        inner[rows, :] = act
        slope_three[rows, :] = slope_of(value, sig)
        value = dot(act, whole(r["w_second"]), NN)
        slope = slope_of(value, sigmoid(value))
        dz_four[rows, :] = (scale * cot[rows, :].astype(F32) * slope).astype(BF16)

    by_tile(edges, block, outward)
    spread(r["second_in0"], dot(inner[...], dz_four[...], TN))
    second = total("second")
    next(second)

    def inward(rows):
        value = dot(dz_four[rows, :], whole(r["w_second"]), NT) * slope_three[rows, :]
        dz_three[rows, :] = value.astype(BF16)

    by_tile(edges, block, inward)
    next(second)
    spread(r["first_in0"], dot(mixed[...], dz_three[...], TN))
    first = total("first")
    next(first)
    dagg = r["dagg"]

    def through(rows):
        value = scale * cot[rows, :].astype(F32) + dot(
            dz_three[rows, :], whole(r["w_first"]), NT
        )
        value = (value * slope_two[rows, :]).astype(BF16)
        dz_two[rows, :] = value

    by_tile(edges, block, through)
    next(first)
    for h in range(subs):
        rows = slice(h * SUB, (h + 1) * SUB)
        dagg[h * width : (h + 1) * width, :] = dot(
            whole(r["w_up"]), dz_two[rows, :], NT
        ).astype(BF16)
    spread(r["up_in0"], dot(agg[...], dz_two[...], NN))
    up = total("up")
    next(up)

    placed, basis_sum = r["placed"], r["basis_sum"]
    basis_sum[...] = jnp.zeros_like(basis_sum)

    def spread_tile(spot):
        src = src_ref[:, spot]
        tgt = tgt_ref[:, spot]
        owner = src // edges
        high = tgt // SUB
        dagg_out = pick(dot(dagg[...], one_hot(SUB, tgt - high * SUB), NN), high, subs, width)
        dcoeff = (dagg_out * din[:, spot].astype(F32)).astype(BF16)
        basis_sum[...] += dot(basis[:, spot], dcoeff, NT)
        coeff = dot(w_basis, basis[:, spot], TN)
        placed[:, spot] = place(dagg_out * coeff, owner, groups)

    by_tile(trips, tile, spread_tile)
    next(second)
    next(up)
    basis_plan = total("basis")
    spread(r["basis_in0"], basis_sum[...])
    next(basis_plan)
    parts, landed = r["parts"], r["landed"]
    b_send, b_recv = sems("bwd")
    back = []
    chunk_sum = r["chunk_sum"]
    calls = {0: (first, second), 1: (up, basis_plan), 2: (first,), 3: ()}
    for c in range(subs):
        chunk_sum[...] = jnp.zeros_like(chunk_sum)

        def scatter_tile(spot):
            src = src_ref[:, spot]
            spots = src - src // edges * edges - c * SUB
            chunk_sum[...] += dot(placed[:, spot], one_hot(SUB, spots), NT)

        by_tile(trips, min(SPAN, trips), scatter_tile)
        back.append([])
        for g in range(groups):
            parts[g, c] = chunk_sum[g * width : (g + 1) * width, :].astype(BF16)
        for k in range(1, groups):
            peer = (me + k) % groups
            cp = remote(
                parts.at[peer, c], landed.at[k, c], b_send.at[k, c], b_recv.at[k, c], {"graph": peer}
            )
            cp.start()
            back[c].append(cp)
        for steps in calls.get(c, ()):
            next(steps)
    for steps in (up, basis_plan):
        next(steps)
    ddown, dz_one, pair_sum = r["ddown"], r["dz_one"], r["pair_sum"]
    cols = dim // 2
    for c in range(subs):
        for cp in back[c]:
            cp.wait()
        value = parts[me, c].astype(F32)
        for k in range(1, groups):
            value = value + landed[k, c].astype(F32)
        value = value.astype(BF16)
        rows = slice(c * SUB, (c + 1) * SUB)
        ddown[:, rows] = value
        slope = z_one[rows, :]
        dz_one[rows, :] = (dot(value, whole(r["w_down"]), ((0,), (1,))) * slope).astype(BF16)
        if c < subs - 1:
            value = dot(feats[rows, :], dz_one[rows, :], TN)
            pair_sum[...] = value if c == 0 else pair_sum[...] + value
    last = slice(edges - SUB, edges)
    for name, part in (("pair_a", slice(0, cols)), ("pair_b", slice(cols, dim))):
        value = dot(feats[last, :], dz_one[last, part], TN)
        if subs > 1:
            value = value + pair_sum[:, part]
        spread(r[name + "_in0"], value)
        if name == "pair_a":
            pair_a = total("pair_a")
            next(pair_a)
    pair_b = total("pair_b")
    next(pair_b)
    next(pair_a)
    spread(r["down_grad_in0"], dot(hidden[...], ddown[...], ((0,), (1,))))
    down_plan = total("down_grad")
    next(down_plan)
    next(pair_b)
    edge = r["edge"]

    def input_grad(rows):
        edge[rows, :] = dot(dz_one[rows, :], whole(w_pair), NT).astype(BF16)

    by_tile(edges // 2, block // 2, input_grad)
    next(pair_a)
    next(down_plan)
    next(pair_b)
    by_tile(edges // 2, block // 2, lambda rows: input_grad(pl.ds(rows.start + edges // 2, rows.size)))
    next(pair_a)
    next(down_plan)
    next(pair_b)
    next(down_plan)
    for steps in (second, first, up, basis_plan, pair_a, pair_b, down_plan):
        for _ in steps:
            pass
    for gather in (early, late):
        gather.drain()


def on_device(
    edge_feats,
    cotangent,
    angle_basis,
    source_edge,
    target_edge,
    pair_weight,
    down_weight,
    basis_weight,
    up_weight,
    res_first,
    res_second,
):
    n = lax.axis_size("dp")
    groups = lax.axis_size("graph")
    edges, dim = edge_feats.shape
    width = down_weight.shape[1]
    trips = source_edge.shape[0]
    subs = edges // SUB
    names, shapes = [], []

    def hold(name, *shape, kind=BF16):
        names.append(name)
        shapes.append(pltpu.VMEM(shape, kind))

    def flags(name, *shape):
        names.extend((name + "_send", name + "_recv"))
        shapes.extend([pltpu.SemaphoreType.DMA(shape)] * 2)

    args = dict(
        feats=edge_feats,
        cot=cotangent,
        basis=angle_basis,
        src=source_edge.reshape(1, -1),
        tgt=target_edge.reshape(1, -1),
        pair=pair_weight,
        down=down_weight,
        wb=basis_weight,
        up=up_weight,
        first=res_first,
        second=res_second,
    )
    outs = {"edge": jax.ShapeDtypeStruct((edges, dim), BF16)}
    plans = {}

    def plan(name, rows, cols, large, kind=BF16):
        shape = (n, groups, rows // (n * groups), cols) if large else (n, rows // n, cols)
        item = jax.ShapeDtypeStruct(shape, kind)
        landing, scratch = total_parts(n, groups, (item,), (large,))
        outs[name + "_out0"] = landing[0]
        hold(name + "_in0", *shape, kind=kind)
        for i, extra in enumerate(scratch):
            names.append(f"{name}_s{i}")
            shapes.append(extra)
        plans[name] = ((large,), len(scratch))

    plan("pair_a", dim, dim // 2, True)
    plan("pair_b", dim, dim // 2, True)
    plan("down_grad", dim, width, False)
    plan("basis", angle_basis.shape[0], width, False, F32)
    plan("up", width, dim, False)
    plan("first", dim, dim, True)
    plan("second", dim, dim, True)
    for name, shard in (
        ("w_pair", pair_weight),
        ("w_down", down_weight),
        ("w_basis", basis_weight),
        ("w_up", up_weight),
        ("w_first", res_first),
        ("w_second", res_second),
    ):
        hold(name, n, *shard.shape)
    for name in ("z_one", "slope_two", "slope_three"):
        hold(name, edges, dim, kind=F32)
    for name in ("hidden", "mixed", "inner", "dz_four", "dz_three", "dz_two", "dz_one"):
        hold(name, edges, dim)
    hold("table", groups, width, edges)
    hold("down_own", subs, width, SUB)
    hold("acc", subs * width, SUB, kind=F32)
    hold("din", width, trips)
    hold("agg", width, edges)
    hold("dagg", subs * width, SUB)
    hold("placed", groups * width, trips)
    hold("basis_sum", angle_basis.shape[0], width, kind=F32)
    hold("chunk_sum", groups * width, SUB, kind=F32)
    hold("parts", groups, subs, width, SUB)
    hold("landed", groups, subs, width, SUB)
    hold("ddown", width, edges)
    count = len(pieces(pair_weight.shape[0])) + 2
    flags("early", n, 3, count)
    names[-1:], shapes[-1:] = ["early_recv"], [pltpu.SemaphoreType.DMA((n, count))]
    hold("pair_sum", dim, dim, kind=F32)
    for name in LOADED:
        hold(name, *args[name].shape, kind=args[name].dtype)
    names.append("loads")
    shapes.append(pltpu.SemaphoreType.DMA((len(LOADED),)))
    flags("late", n, 3, 3)
    names[-1:], shapes[-1:] = ["late_recv"], [pltpu.SemaphoreType.DMA((n, 3))]
    flags("fwd", groups, subs)
    flags("bwd", groups, subs)
    firsts = [name + "_far" if name in LOADED else name for name in args]
    results = pl.pallas_call(
        functools.partial(block_kernel, n, groups, firsts + list(outs) + names, plans),
        out_shape=list(outs.values()),
        in_specs=[ANY if name in LOADED else VM for name in args],
        out_specs=[VM] * len(outs),
        scratch_shapes=shapes,
        compiler_params=pltpu.CompilerParams(collective_id=0, has_side_effects=True),
        name="block",
    )(*args.values())
    got = dict(zip(outs, results))
    return write_grads(got, groups)


def write_kernel(ins, outs, *refs):
    landed = dict(zip(ins, refs))
    for name, out in zip(outs, refs[len(ins) :]):
        if name == "edge":
            out[...] = landed["edge"][...]
            continue
        col = 0
        for part in (name,) if name in landed else (name + "_a", name + "_b"):
            item = landed[part]
            groups, rows, cols = item.shape
            spot = slice(col, col + cols)
            col += cols
            if name in SHARED:
                value = item[0].astype(F32)
                for g in range(1, groups):
                    value = value + item[g].astype(F32)
                out[:, spot] = value
            else:
                for g in range(groups):
                    out[g * rows : (g + 1) * rows, spot] = item[g].astype(F32)


SHARED = ("down_grad", "basis", "up")


def write_grads(got, groups):
    got = {name.removesuffix("_out0"): item for name, item in got.items()}
    dim = got["edge"].shape[1]
    outs = {"edge": jax.ShapeDtypeStruct(got["edge"].shape, BF16)}
    for name in ("pair", "down_grad", "basis", "up", "first", "second"):
        item = got[name] if name in got else got[name + "_a"]
        rows = item.shape[1] * (1 if name in SHARED else groups)
        cols = item.shape[2] if name in got else dim
        outs[name] = jax.ShapeDtypeStruct((rows, cols), F32)
    return tuple(
        pl.pallas_call(
            functools.partial(write_kernel, list(got), list(outs)),
            out_shape=list(outs.values()),
            in_specs=[VM] * len(got),
            out_specs=[VM] * len(outs),
            name="write_grads",
        )(*got.values())
    )


def solution(mesh):
    return jax.shard_map(
        on_device,
        mesh=mesh,
        in_specs=(
            P(("dp", "graph"), None),
            P(("dp", "graph"), None),
            P(None, ("dp", "graph")),
            P(("dp", "graph")),
            P(("dp", "graph")),
            P("dp", None),
            P("dp", None),
            P("dp", None),
            P("dp", None),
            P("dp", None),
            P("dp", None),
        ),
        out_specs=(
            P(("dp", "graph"), None),
            P("dp", None),
            P("dp", None),
            P("dp", None),
            P("dp", None),
            P("dp", None),
            P("dp", None),
        ),
        check_vma=False,
    )
```

```python
import functools
import math

import jax
import jax.numpy as jnp
from jax import lax
from jax.experimental import pallas as pl
from jax.experimental.pallas import tpu as pltpu
from jax.sharding import PartitionSpec as P

MESH = pl.DeviceIdType.MESH
F32 = jnp.float32
BF16 = jnp.bfloat16
VM = pl.BlockSpec(memory_space=pltpu.VMEM)
ANY = pl.BlockSpec(memory_space=pl.ANY)
SUB = 256
TILE = 2048
SPAN = 2048
PASSES = 2
LOADED = ("feats", "basis", "src", "tgt", "cot")
PIECE = 16
ROWS = 512


def remote(src, dst, send, recv, target):
    return pltpu.make_async_remote_copy(
        src_ref=src,
        dst_ref=dst,
        send_sem=send,
        recv_sem=recv,
        device_id=target,
        device_id_type=MESH,
    )


def sigmoid(value):
    return 0.5 * jnp.tanh(0.5 * value) + 0.5


def slope_of(value, sig):
    return sig * (1.0 + value * (1.0 - sig))


def greet(targets, waits):
    barrier = pltpu.get_barrier_semaphore()
    for target in targets:
        pl.semaphore_signal(barrier, inc=1, device_id=target, device_id_type=MESH)
    pl.semaphore_wait(barrier, waits)


def graph_peers(groups):
    me = lax.axis_index("graph")
    return [{"graph": (me + k) % groups} for k in range(1, groups)]


def chip_peers(n):
    half = n // 2
    dp = lax.axis_index("dp")
    return [{"dp": (dp // 2 + k) % half * 2 + dp % 2} for k in range(1, half)]


def core_peer():
    dp = lax.axis_index("dp")
    return [{"dp": dp + 1 - 2 * (dp % 2)}]


def flag_count(n, groups, large):
    return (groups if large else 1) + n // 2 - 1 + groups - 1


def total_steps(n, groups, large, src, out, scratch, send, recv):
    half = n // 2
    dp = lax.axis_index("dp")
    me = lax.axis_index("graph")
    pos = dp // 2
    core = dp % 2
    at_c = groups if large else 1
    at_d = at_c + half - 1
    got, summed, arrived, done = scratch[:4]
    sent = []

    def start(block, landing, at, target):
        cp = remote(block, landing, send(at), recv.at[at], target)
        cp.start()
        sent.append(cp)
        return cp

    first = start(src.at[1 - core], got, 0, {"dp": dp + 1 - 2 * core})
    yield
    first.wait_recv()
    second = []
    for q in range(half):
        value = (src[core, q].astype(F32) + got[q].astype(F32)).astype(summed.dtype)
        if large:
            summed[:, q] = value
        else:
            summed[q] = value
    if large:
        for k in range(1, groups):
            peer = (me + k) % groups
            second.append(start(summed.at[peer], scratch[4].at[k], k, {"graph": peer}))
    yield
    part = summed
    if large:
        for cp in second:
            cp.wait_recv()
        value = summed[me].astype(F32)
        for k in range(1, groups):
            value = value + scratch[4][k].astype(F32)
        part = scratch[5]
        part[...] = value.astype(part.dtype)
    third = []
    for k in range(1, half):
        chip = (pos + k) % half
        third.append(
            start(part.at[chip], arrived.at[k], at_c + k - 1, {"dp": chip * 2 + core})
        )
    yield
    for cp in third:
        cp.wait_recv()
    value = part[pos].astype(F32)
    for k in range(1, half):
        value = value + arrived[k].astype(F32)
    value = value.astype(done.dtype)
    done[...] = value
    fourth = []
    for k in range(1, groups):
        fourth.append(
            start(done, out.at[me], at_d + k - 1, {"graph": (me + k) % groups})
        )
    out[me] = value
    yield
    for cp in fourth:
        cp.wait_recv()
    for cp in sent:
        cp.wait_send()


def total_parts(n, groups, shape, large, kind):
    half = n // 2
    tail = shape[3:] if large else shape[2:]
    scratch = [
        shape[1:],
        ((groups, half) if large else (half,)) + tail,
        (half,) + tail,
        tail,
    ]
    if large:
        scratch += [(groups, half) + tail, (half,) + tail]
    out = jax.ShapeDtypeStruct((groups,) + tail, kind)
    return out, [pltpu.VMEM(item, kind) for item in scratch]


def greet_all(n, groups):
    greet(core_peer() + graph_peers(groups) + chip_peers(n), groups + n // 2 - 1)


def one_hot(size, row):
    spots = lax.broadcasted_iota(jnp.int32, (size, row.shape[1]), 0)
    return jnp.where(spots == row, 1.0, 0.0).astype(BF16)


def pick(stack, owner, groups, width):
    value = jnp.where(owner == 0, stack[:width], 0.0)
    for g in range(1, groups):
        value = value + jnp.where(owner == g, stack[g * width : (g + 1) * width], 0.0)
    return value


def place(value, owner, groups):
    return jnp.concatenate(
        [jnp.where(owner == g, value, 0.0).astype(BF16) for g in range(groups)], axis=0
    )


def dot(a, b, dims):
    return lax.dot_general(a, b, (dims, ((), ())), preferred_element_type=F32)


NN = ((1,), (0,))
NT = ((1,), (1,))
TN = ((0,), (0,))


class Gather:
    def __init__(self, n, ins, outs, send, base, recv):
        self.ins, self.outs, self.send, self.base, self.recv = ins, outs, send, base, recv
        self.count = len(ins)
        self.half = n // 2
        self.dp = lax.axis_index("dp")
        self.pos = self.dp // 2
        self.core = self.dp % 2
        self.partner = self.dp + 1 - 2 * self.core
        self.has_up = self.pos < self.half - 1
        self.has_down = self.pos > 0

    def copy(self, w, src, shard, way, target):
        return remote(
            src,
            self.outs[w].at[shard],
            self.send.at[self.base + (shard // 2 * 3 + way) * self.count + w],
            self.recv.at[shard, w],
            {"dp": target},
        )

    def pass_on(self, w, src, shard, way):
        target = (self.dp + 2, self.dp - 2, self.partner)[way]
        self.copy(w, src, shard, way, target).start()

    def start(self):
        for w in range(self.count):
            src = self.ins[w]

            @pl.when(self.has_up)
            def _():
                self.pass_on(w, src, self.dp, 0)

            @pl.when(self.has_down)
            def _():
                self.pass_on(w, src, self.dp, 1)

            self.pass_on(w, src, self.dp, 2)
        for w in range(self.count):
            self.outs[w][self.dp] = self.ins[w][...]

    def arrive(self, w, shard):
        self.copy(w, self.outs[w].at[shard], shard, 2, self.partner).wait_recv()

    def hop(self, k):
        for w in range(self.count):

            @pl.when(self.pos >= k)
            def _():
                shard = self.dp - 2 * k
                self.arrive(w, shard)

                @pl.when(self.has_up)
                def _():
                    self.pass_on(w, self.outs[w].at[shard], shard, 0)

                self.pass_on(w, self.outs[w].at[shard], shard, 2)

            @pl.when(self.pos + k < self.half)
            def _():
                shard = self.dp + 2 * k
                self.arrive(w, shard)

                @pl.when(self.has_down)
                def _():
                    self.pass_on(w, self.outs[w].at[shard], shard, 1)

                self.pass_on(w, self.outs[w].at[shard], shard, 2)

    def across(self, k):
        for w in range(self.count):
            if k == 0:
                self.arrive(w, self.partner)
                continue

            @pl.when(self.pos >= k)
            def _():
                self.arrive(w, self.partner - 2 * k)

            @pl.when(self.pos + k < self.half)
            def _():
                self.arrive(w, self.partner + 2 * k)

    def drain(self):
        for w in range(self.count):
            for q in range(self.half):
                mine = 2 * q + self.core
                block = self.outs[w].at[mine]
                self.copy(w, block, mine, 2, self.partner).wait_send()

                @pl.when(jnp.logical_and(self.pos >= q, self.has_up))
                def _():
                    self.copy(w, block, mine, 0, self.dp + 2).wait_send()

                @pl.when(jnp.logical_and(self.pos <= q, self.has_down))
                def _():
                    self.copy(w, block, mine, 1, self.dp - 2).wait_send()


def pieces(rows):
    size = PIECE if rows % PIECE == 0 else rows
    return [pl.ds(i * size, size) for i in range(rows // size)]


def whole(ref):
    value = ref[...]
    return value.reshape(-1, value.shape[2])


def spread(ref, value):
    value = value.astype(ref.dtype)
    groups = ref.shape[2] if len(ref.shape) == 5 else 1
    rows = ref.shape[-2]
    for i in range(ref.shape[0] * ref.shape[1] * groups):
        part = value[i * rows : (i + 1) * rows]
        dp = i // groups
        if len(ref.shape) == 5:
            ref[dp % 2, dp // 2, i % groups] = part
        else:
            ref[dp % 2, dp // 2] = part


def by_tile(total, tile, body):
    def step(i, carry):
        body(pl.ds(pl.multiple_of(i * tile, tile), tile))
        return carry

    lax.fori_loop(0, total // tile, step, 0)


def block_kernel(n, groups, names, plans, *refs):
    r = dict(zip(names, refs))
    feats, cot, basis = r["feats"], r["cot"], r["basis"]
    src_ref, tgt_ref = r["src"], r["tgt"]
    z_one, hidden, table, acc = r["z_one"], r["hidden"], r["table"], r["acc"]
    edges, dim = feats.shape
    width = r["down"].shape[1]
    trips = src_ref.shape[1]
    subs = edges // SUB
    half = n // 2
    scale = math.sqrt(0.5)
    me = lax.axis_index("graph")
    tile = min(TILE, trips)
    tiles = trips // tile

    spare = [0]

    def take(count):
        low = spare[0]
        spare[0] += count
        return lambda i: r["sends"].at[low + i]

    def total(name):
        large, count = plans[name]
        return total_steps(
            n,
            groups,
            large,
            r[name + "_in"],
            r[name + "_out"],
            [r[f"{name}_s{i}"] for i in range(count)],
            take(flag_count(n, groups, large)),
            r[name + "_recv"],
        )

    loads = {}
    for i, name in enumerate(LOADED):
        loads[name] = pltpu.make_async_copy(r[name + "_far"], r[name], r["loads"].at[i])
        loads[name].start()
    greet_all(n, groups)
    cuts = pieces(r["pair"].shape[0])
    early = Gather(
        n,
        [r["pair"].at[rows] for rows in cuts] + [r["down"], r["wb"]],
        [r["w_pair"].at[:, rows] for rows in cuts] + [r["w_down"], r["w_basis"]],
        r["sends"],
        0,
        r["early_recv"],
    )
    late = Gather(
        n,
        (r["up"], r["first"], r["second"]),
        (r["w_up"], r["w_first"], r["w_second"]),
        r["sends"],
        early.count * half * 3,
        r["late_recv"],
    )
    early.start()
    w_pair = r["w_pair"]
    for k in range(1, half):
        early.hop(k)
    late.start()
    for k in range(half):
        early.across(k)
    loads["feats"].wait()
    down_own = r["down_own"]
    f_send, f_recv = r["fwd_send"], r["fwd_recv"]
    ahead = []
    for c in range(subs):
        rows = slice(c * SUB, (c + 1) * SUB)
        value = dot(feats[rows, :], whole(w_pair), NN)
        sig = sigmoid(value)
        act = (value * sig).astype(BF16)
        hidden[rows, :] = act
        down_own[c] = dot(whole(r["w_down"]), act, ((0,), (1,))).astype(BF16)
        table[me, :, rows] = down_own[c]
        ahead.append([])
        for k in range(1, groups):
            cp = remote(
                down_own.at[c],
                table.at[me, :, rows],
                f_send.at[k - 1, c],
                f_recv.at[k - 1, c],
                {"graph": (me + k) % groups},
            )
            cp.start()
            ahead[c].append(cp)
        z_one[rows, :] = slope_of(value, sig)
    acc[...] = jnp.zeros_like(acc)
    w_basis = whole(r["w_basis"])
    din = r["din"]
    reach = edges // PASSES
    for name in ("basis", "src", "tgt"):
        loads[name].wait()

    def gather_tile(part, i, carry):
        spot = pl.ds(pl.multiple_of(i * tile, tile), tile)
        src = src_ref[:, spot]
        owner = src // edges
        cols = slice(part * reach, (part + 1) * reach)
        stack = dot(
            table[:, :, cols].reshape(groups * width, reach),
            one_hot(reach, src - owner * edges - part * reach),
            NN,
        )
        down_in = pick(stack, owner, groups, width)
        if part > 0:
            down_in = down_in + din[:, spot].astype(F32)
        din[:, spot] = down_in.astype(BF16)
        if part == PASSES - 1:
            tgt = tgt_ref[:, spot]
            coeff = dot(w_basis, basis[:, spot], TN)
            high = tgt // SUB
            acc[...] += dot(
                place(down_in * coeff, high, subs), one_hot(SUB, tgt - high * SUB), NT
            )
        return carry

    units = PASSES * tiles
    stops = {max(units * k // half - 1, 0): k for k in range(1, half)}
    for part in range(PASSES):
        for c in range(subs * part // PASSES, subs * (part + 1) // PASSES):
            for cp in ahead[c]:
                cp.wait()
        low = 0
        for unit in range(tiles):
            if part * tiles + unit in stops:
                lax.fori_loop(low, unit, functools.partial(gather_tile, part), 0)
                low = unit
                late.hop(stops[part * tiles + unit])
        lax.fori_loop(low, tiles, functools.partial(gather_tile, part), 0)
    late.across(0)
    agg = r["agg"]
    for h in range(subs):
        agg[:, h * SUB : (h + 1) * SUB] = acc[h * width : (h + 1) * width, :].astype(BF16)
    for k in range(1, half):
        late.across(k)

    for gather in (early, late):
        gather.drain()
    loads["cot"].wait()
    mixed, inner = r["mixed"], r["inner"]
    slope_two, slope_three = r["slope_two"], r["slope_three"]
    dz_four, dz_three, dz_two = r["dz_four"], r["dz_three"], r["dz_two"]
    block = min(ROWS, edges)

    def outward(rows):
        value = dot(agg[:, rows], whole(r["w_up"]), TN)
        sig = sigmoid(value)
        act = (value * sig).astype(BF16)
        mixed[rows, :] = act
        slope_two[rows, :] = slope_of(value, sig)
        value = dot(act, whole(r["w_first"]), NN)
        sig = sigmoid(value)
        act = (value * sig).astype(BF16)
        inner[rows, :] = act
        slope_three[rows, :] = slope_of(value, sig)
        value = dot(act, whole(r["w_second"]), NN)
        slope = slope_of(value, sigmoid(value))
        dz_four[rows, :] = (scale * cot[rows, :].astype(F32) * slope).astype(BF16)

    by_tile(edges, block, outward)
    spread(r["second_in"], dot(inner[...], dz_four[...], TN))
    second = total("second")
    next(second)

    def inward(rows):
        value = dot(dz_four[rows, :], whole(r["w_second"]), NT) * slope_three[rows, :]
        dz_three[rows, :] = value.astype(BF16)

    by_tile(edges, block, inward)
    next(second)
    spread(r["first_in"], dot(mixed[...], dz_three[...], TN))
    first = total("first")
    next(first)
    dagg = r["dagg"]

    def through(rows):
        value = scale * cot[rows, :].astype(F32) + dot(
            dz_three[rows, :], whole(r["w_first"]), NT
        )
        value = (value * slope_two[rows, :]).astype(BF16)
        dz_two[rows, :] = value

    by_tile(edges, block, through)
    next(first)
    for h in range(subs):
        rows = slice(h * SUB, (h + 1) * SUB)
        dagg[h * width : (h + 1) * width, :] = dot(
            whole(r["w_up"]), dz_two[rows, :], NT
        ).astype(BF16)
    spread(r["up_in"], dot(agg[...], dz_two[...], NN))
    up = total("up")
    next(up)

    placed, basis_sum = r["placed"], r["basis_sum"]
    basis_sum[...] = jnp.zeros_like(basis_sum)

    def spread_tile(spot):
        src = src_ref[:, spot]
        tgt = tgt_ref[:, spot]
        owner = src // edges
        high = tgt // SUB
        dagg_out = pick(dot(dagg[...], one_hot(SUB, tgt - high * SUB), NN), high, subs, width)
        dcoeff = (dagg_out * din[:, spot].astype(F32)).astype(BF16)
        basis_sum[...] += dot(basis[:, spot], dcoeff, NT)
        coeff = dot(w_basis, basis[:, spot], TN)
        placed[:, spot] = place(dagg_out * coeff, owner, groups)

    by_tile(trips, tile, spread_tile)
    next(second)
    next(up)
    basis_plan = total("basis")
    spread(r["basis_in"], basis_sum[...])
    next(basis_plan)
    parts, landed = r["parts"], r["landed"]
    b_send, b_recv = take((groups - 1) * subs), r["bwd_recv"]
    back = []
    chunk_sum = r["chunk_sum"]
    calls = {1: (second, first, up, basis_plan, basis_plan)}
    for c in range(subs):
        chunk_sum[...] = jnp.zeros_like(chunk_sum)

        def scatter_tile(spot):
            src = src_ref[:, spot]
            spots = src - src // edges * edges - c * SUB
            chunk_sum[...] += dot(placed[:, spot], one_hot(SUB, spots), NT)

        by_tile(trips, min(SPAN, trips), scatter_tile)
        back.append([])
        for g in range(groups):
            parts[g, c] = chunk_sum[g * width : (g + 1) * width, :].astype(BF16)
        for k in range(1, groups):
            peer = (me + k) % groups
            cp = remote(
                parts.at[peer, c], landed.at[k, c], b_send((k - 1) * subs + c), b_recv.at[k - 1, c], {"graph": peer}
            )
            cp.start()
            back[c].append(cp)
        for steps in calls.get(c, ()):
            next(steps)
    for steps in (first, up, basis_plan):
        next(steps)
    ddown, dz_one, pair_sum = r["ddown"], r["dz_one"], r["pair_sum"]
    cols = dim // 2
    for c in range(subs):
        for cp in back[c]:
            cp.wait()
        value = parts[me, c].astype(F32)
        for k in range(1, groups):
            value = value + landed[k, c].astype(F32)
        value = value.astype(BF16)
        rows = slice(c * SUB, (c + 1) * SUB)
        ddown[:, rows] = value
        slope = z_one[rows, :]
        dz_one[rows, :] = (dot(value, whole(r["w_down"]), ((0,), (1,))) * slope).astype(BF16)
        if c < subs - 1:
            value = dot(feats[rows, :], dz_one[rows, :], TN)
            pair_sum[...] = value if c == 0 else pair_sum[...] + value
    last = slice(edges - SUB, edges)
    for name, part in (("pair_a", slice(0, cols)), ("pair_b", slice(cols, dim))):
        value = dot(feats[last, :], dz_one[last, part], TN)
        if subs > 1:
            value = value + pair_sum[:, part]
        spread(r[name + "_in"], value)
        if name == "pair_a":
            pair_a = total("pair_a")
            next(pair_a)
    pair_b = total("pair_b")
    next(pair_b)
    next(pair_a)
    spread(r["down_grad_in"], dot(hidden[...], ddown[...], ((0,), (1,))))
    down_plan = total("down_grad")
    next(down_plan)
    next(pair_b)
    edge = r["edge"]

    def input_grad(rows):
        edge[rows, :] = dot(dz_one[rows, :], whole(w_pair), NT).astype(BF16)

    by_tile(edges // 2, block // 2, input_grad)
    next(down_plan)
    next(down_plan)
    next(pair_a)
    next(pair_b)
    by_tile(
        edges // 2, block // 2, lambda rows: input_grad(pl.ds(rows.start + edges // 2, rows.size))
    )
    next(down_plan)
    next(pair_a)
    next(pair_b)
    for steps in (second, first, up, basis_plan, pair_a, pair_b, down_plan):
        for _ in steps:
            pass


def on_device(
    edge_feats,
    cotangent,
    angle_basis,
    source_edge,
    target_edge,
    pair_weight,
    down_weight,
    basis_weight,
    up_weight,
    res_first,
    res_second,
):
    n = lax.axis_size("dp")
    groups = lax.axis_size("graph")
    edges, dim = edge_feats.shape
    width = down_weight.shape[1]
    trips = source_edge.shape[0]
    subs = edges // SUB
    names, shapes = [], []

    def hold(name, *shape, kind=BF16):
        names.append(name)
        shapes.append(pltpu.VMEM(shape, kind))

    def flags(name, *shape):
        names.append(name)
        shapes.append(pltpu.SemaphoreType.DMA(shape))

    args = dict(
        feats=edge_feats,
        cot=cotangent,
        basis=angle_basis,
        src=source_edge.reshape(1, -1),
        tgt=target_edge.reshape(1, -1),
        pair=pair_weight,
        down=down_weight,
        wb=basis_weight,
        up=up_weight,
        first=res_first,
        second=res_second,
    )
    outs = {"edge": jax.ShapeDtypeStruct((edges, dim), BF16)}
    plans, used = {}, []

    def plan(name, rows, cols, large, kind=BF16):
        lead = (2, n // 2, groups) if large else (2, n // 2)
        shape = lead + (rows // (n * groups if large else n), cols)
        landing, scratch = total_parts(n, groups, shape, large, kind)
        outs[name + "_out"] = landing
        hold(name + "_in", *shape, kind=kind)
        for i, extra in enumerate(scratch):
            names.append(f"{name}_s{i}")
            shapes.append(extra)
        size = flag_count(n, groups, large)
        flags(name + "_recv", size)
        plans[name] = (large, len(scratch))
        used.append(size)

    plan("pair_a", dim, dim // 2, True)
    plan("pair_b", dim, dim // 2, True)
    plan("down_grad", dim, width, False)
    plan("basis", angle_basis.shape[0], width, False, F32)
    plan("up", width, dim, False)
    plan("first", dim, dim, True)
    plan("second", dim, dim, True)
    for name, shard in (
        ("w_pair", pair_weight),
        ("w_down", down_weight),
        ("w_basis", basis_weight),
        ("w_up", up_weight),
        ("w_first", res_first),
        ("w_second", res_second),
    ):
        hold(name, n, *shard.shape)
    for name in ("z_one", "slope_two", "slope_three"):
        hold(name, edges, dim, kind=F32)
    for name in ("hidden", "mixed", "inner", "dz_four", "dz_three", "dz_two", "dz_one"):
        hold(name, edges, dim)
    hold("table", groups, width, edges)
    hold("down_own", subs, width, SUB)
    hold("acc", subs * width, SUB, kind=F32)
    hold("din", width, trips)
    hold("agg", width, edges)
    hold("dagg", subs * width, SUB)
    hold("placed", groups * width, trips)
    hold("basis_sum", angle_basis.shape[0], width, kind=F32)
    hold("chunk_sum", groups * width, SUB, kind=F32)
    hold("parts", groups, subs, width, SUB)
    hold("landed", groups, subs, width, SUB)
    hold("ddown", width, edges)
    count = len(pieces(pair_weight.shape[0])) + 2
    flags("early_recv", n, count)
    flags("late_recv", n, 3)
    used.append((groups - 1) * subs)
    flags("sends", max(n // 2 * 3 * (count + 3), sum(used)))
    for name in ("fwd_send", "fwd_recv", "bwd_recv"):
        flags(name, groups - 1, subs)
    hold("pair_sum", dim, dim, kind=F32)
    for name in LOADED:
        hold(name, *args[name].shape, kind=args[name].dtype)
    names.append("loads")
    shapes.append(pltpu.SemaphoreType.DMA((len(LOADED),)))
    firsts = [name + "_far" if name in LOADED else name for name in args]
    results = pl.pallas_call(
        functools.partial(block_kernel, n, groups, firsts + list(outs) + names, plans),
        out_shape=list(outs.values()),
        in_specs=[ANY if name in LOADED else VM for name in args],
        out_specs=[VM] * len(outs),
        scratch_shapes=shapes,
        compiler_params=pltpu.CompilerParams(collective_id=0, has_side_effects=True),
        name="block",
    )(*args.values())
    got = dict(zip(outs, results))
    return write_grads(got, groups)


def write_kernel(ins, outs, *refs):
    landed = dict(zip(ins, refs))
    for name, out in zip(outs, refs[len(ins) :]):
        if name == "edge":
            out[...] = landed["edge"][...]
            continue
        col = 0
        for part in (name,) if name in landed else (name + "_a", name + "_b"):
            item = landed[part]
            groups, rows, cols = item.shape
            spot = slice(col, col + cols)
            col += cols
            if name in SHARED:
                value = item[0].astype(F32)
                for g in range(1, groups):
                    value = value + item[g].astype(F32)
                out[:, spot] = value
            else:
                for g in range(groups):
                    out[g * rows : (g + 1) * rows, spot] = item[g].astype(F32)


SHARED = ("down_grad", "basis", "up")


def write_grads(got, groups):
    got = {name.removesuffix("_out"): item for name, item in got.items()}
    dim = got["edge"].shape[1]
    outs = {"edge": jax.ShapeDtypeStruct(got["edge"].shape, BF16)}
    for name in ("pair", "down_grad", "basis", "up", "first", "second"):
        item = got[name] if name in got else got[name + "_a"]
        rows = item.shape[1] * (1 if name in SHARED else groups)
        cols = item.shape[2] if name in got else dim
        outs[name] = jax.ShapeDtypeStruct((rows, cols), F32)
    return tuple(
        pl.pallas_call(
            functools.partial(write_kernel, list(got), list(outs)),
            out_shape=list(outs.values()),
            in_specs=[VM] * len(got),
            out_specs=[VM] * len(outs),
            name="write_grads",
        )(*got.values())
    )


def solution(mesh):
    return jax.shard_map(
        on_device,
        mesh=mesh,
        in_specs=(
            P(("dp", "graph"), None),
            P(("dp", "graph"), None),
            P(None, ("dp", "graph")),
            P(("dp", "graph")),
            P(("dp", "graph")),
            P("dp", None),
            P("dp", None),
            P("dp", None),
            P("dp", None),
            P("dp", None),
            P("dp", None),
        ),
        out_specs=(
            P(("dp", "graph"), None),
            P("dp", None),
            P("dp", None),
            P("dp", None),
            P("dp", None),
            P("dp", None),
            P("dp", None),
        ),
        check_vma=False,
    )
```

```python
import functools
import math
import types

import jax
import jax.numpy as jnp
from jax import lax
from jax.experimental import pallas as pl
from jax.experimental.pallas import tpu as pltpu
from jax.sharding import PartitionSpec as P

MESH = pl.DeviceIdType.MESH
F32 = jnp.float32
BF16 = jnp.bfloat16
VM = pl.BlockSpec(memory_space=pltpu.VMEM)
ANY = pl.BlockSpec(memory_space=pl.ANY)
SUB = 256
TILE = 2048
SPAN = 2048
PASSES = 2
LOADED = ("feats", "basis", "src", "tgt", "cot")
PIECE = 16
ROWS = 512


def remote(src, dst, send, recv, target):
    return pltpu.make_async_remote_copy(
        src_ref=src,
        dst_ref=dst,
        send_sem=send,
        recv_sem=recv,
        device_id=target,
        device_id_type=MESH,
    )


def sigmoid(value):
    return 0.5 * jnp.tanh(0.5 * value) + 0.5


def slope_of(value, sig):
    return sig * (1.0 + value * (1.0 - sig))


def greet(targets, waits):
    barrier = pltpu.get_barrier_semaphore()
    for target in targets:
        pl.semaphore_signal(barrier, inc=1, device_id=target, device_id_type=MESH)
    pl.semaphore_wait(barrier, waits)


def graph_peers(groups):
    me = lax.axis_index("graph")
    return [{"graph": (me + k) % groups} for k in range(1, groups)]


def chip_peers(n):
    half = n // 2
    dp = lax.axis_index("dp")
    return [{"dp": (dp // 2 + k) % half * 2 + dp % 2} for k in range(1, half)]


def core_peer():
    dp = lax.axis_index("dp")
    return [{"dp": dp + 1 - 2 * (dp % 2)}]


def flag_count(n, groups, large):
    return (groups if large else 1) + n // 2 - 1 + groups - 1


def total_steps(n, groups, large, src, out, scratch, send, recv):
    half = n // 2
    dp = lax.axis_index("dp")
    me = lax.axis_index("graph")
    pos = dp // 2
    core = dp % 2
    at_c = groups if large else 1
    at_d = at_c + half - 1
    got, summed, arrived, done = scratch[:4]
    sent = []

    def start(block, landing, at, target):
        cp = remote(block, landing, send(at), recv.at[at], target)
        cp.start()
        sent.append(cp)
        return cp

    first = start(src.at[1 - core], got, 0, {"dp": dp + 1 - 2 * core})
    yield
    first.wait_recv()
    second = []
    for q in range(half):
        value = (src[core, q].astype(F32) + got[q].astype(F32)).astype(summed.dtype)
        if large:
            summed[:, q] = value
        else:
            summed[q] = value
    if large:
        for k in range(1, groups):
            peer = (me + k) % groups
            second.append(start(summed.at[peer], scratch[4].at[k], k, {"graph": peer}))
    yield
    part = summed
    if large:
        for cp in second:
            cp.wait_recv()
        value = summed[me].astype(F32)
        for k in range(1, groups):
            value = value + scratch[4][k].astype(F32)
        part = scratch[5]
        part[...] = value.astype(part.dtype)
    third = []
    for k in range(1, half):
        chip = (pos + k) % half
        third.append(
            start(part.at[chip], arrived.at[k], at_c + k - 1, {"dp": chip * 2 + core})
        )
    yield
    for cp in third:
        cp.wait_recv()
    value = part[pos].astype(F32)
    for k in range(1, half):
        value = value + arrived[k].astype(F32)
    value = value.astype(done.dtype)
    done[...] = value
    fourth = []
    for k in range(1, groups):
        fourth.append(
            start(done, out.at[me], at_d + k - 1, {"graph": (me + k) % groups})
        )
    out[me] = value
    yield
    for cp in fourth:
        cp.wait_recv()
    for cp in sent:
        cp.wait_send()


def total_parts(n, groups, shape, large, kind):
    half = n // 2
    tail = shape[3:] if large else shape[2:]
    scratch = [
        shape[1:],
        ((groups, half) if large else (half,)) + tail,
        (half,) + tail,
        tail,
    ]
    if large:
        scratch += [(groups, half) + tail, (half,) + tail]
    out = jax.ShapeDtypeStruct((groups,) + tail, kind)
    return out, [pltpu.VMEM(item, kind) for item in scratch]


def greet_all(n, groups):
    greet(core_peer() + graph_peers(groups) + chip_peers(n), groups + n // 2 - 1)


def one_hot(size, row):
    spots = lax.broadcasted_iota(jnp.int32, (size, row.shape[1]), 0)
    return jnp.where(spots == row, 1.0, 0.0).astype(BF16)


def pick(stack, owner, groups, width):
    value = jnp.where(owner == 0, stack[:width], 0.0)
    for g in range(1, groups):
        value = value + jnp.where(owner == g, stack[g * width : (g + 1) * width], 0.0)
    return value


def place(value, owner, groups):
    return jnp.concatenate(
        [jnp.where(owner == g, value, 0.0).astype(BF16) for g in range(groups)], axis=0
    )


def dot(a, b, dims):
    return lax.dot_general(a, b, (dims, ((), ())), preferred_element_type=F32)


NN = ((1,), (0,))
NT = ((1,), (1,))
TN = ((0,), (0,))


class Gather:
    def __init__(self, n, ins, outs, send, base, recv):
        self.ins, self.outs, self.send, self.base, self.recv = ins, outs, send, base, recv
        self.count = len(ins)
        self.half = n // 2
        self.dp = lax.axis_index("dp")
        self.pos = self.dp // 2
        self.core = self.dp % 2
        self.partner = self.dp + 1 - 2 * self.core
        self.has_up = self.pos < self.half - 1
        self.has_down = self.pos > 0

    def copy(self, w, src, shard, way, target):
        return remote(
            src,
            self.outs[w].at[shard],
            self.send.at[self.base + (shard // 2 * 3 + way) * self.count + w],
            self.recv.at[shard, w],
            {"dp": target},
        )

    def pass_on(self, w, src, shard, way):
        target = (self.dp + 2, self.dp - 2, self.partner)[way]
        self.copy(w, src, shard, way, target).start()

    def start(self):
        for w in range(self.count):
            src = self.ins[w]

            @pl.when(self.has_up)
            def _():
                self.pass_on(w, src, self.dp, 0)

            @pl.when(self.has_down)
            def _():
                self.pass_on(w, src, self.dp, 1)

            self.pass_on(w, src, self.dp, 2)
        for w in range(self.count):
            self.outs[w][self.dp] = self.ins[w][...]

    def arrive(self, w, shard):
        self.copy(w, self.outs[w].at[shard], shard, 2, self.partner).wait_recv()

    def hop(self, k):
        for w in range(self.count):

            @pl.when(self.pos >= k)
            def _():
                shard = self.dp - 2 * k
                self.arrive(w, shard)

                @pl.when(self.has_up)
                def _():
                    self.pass_on(w, self.outs[w].at[shard], shard, 0)

                self.pass_on(w, self.outs[w].at[shard], shard, 2)

            @pl.when(self.pos + k < self.half)
            def _():
                shard = self.dp + 2 * k
                self.arrive(w, shard)

                @pl.when(self.has_down)
                def _():
                    self.pass_on(w, self.outs[w].at[shard], shard, 1)

                self.pass_on(w, self.outs[w].at[shard], shard, 2)

    def across(self, k):
        for w in range(self.count):
            if k == 0:
                self.arrive(w, self.partner)
                continue

            @pl.when(self.pos >= k)
            def _():
                self.arrive(w, self.partner - 2 * k)

            @pl.when(self.pos + k < self.half)
            def _():
                self.arrive(w, self.partner + 2 * k)

    def drain(self):
        for w in range(self.count):
            for q in range(self.half):
                mine = 2 * q + self.core
                block = self.outs[w].at[mine]
                self.copy(w, block, mine, 2, self.partner).wait_send()

                @pl.when(jnp.logical_and(self.pos >= q, self.has_up))
                def _():
                    self.copy(w, block, mine, 0, self.dp + 2).wait_send()

                @pl.when(jnp.logical_and(self.pos <= q, self.has_down))
                def _():
                    self.copy(w, block, mine, 1, self.dp - 2).wait_send()


def pieces(rows):
    size = PIECE if rows % PIECE == 0 else rows
    return [pl.ds(i * size, size) for i in range(rows // size)]


def whole(ref):
    value = ref[...]
    return value.reshape(-1, value.shape[2])


def spread(ref, value):
    value = value.astype(ref.dtype)
    groups = ref.shape[2] if len(ref.shape) == 5 else 1
    rows = ref.shape[-2]
    for i in range(ref.shape[0] * ref.shape[1] * groups):
        part = value[i * rows : (i + 1) * rows]
        dp = i // groups
        if len(ref.shape) == 5:
            ref[dp % 2, dp // 2, i % groups] = part
        else:
            ref[dp % 2, dp // 2] = part


def by_tile(total, tile, body):
    def step(i, carry):
        body(pl.ds(pl.multiple_of(i * tile, tile), tile))
        return carry

    lax.fori_loop(0, total // tile, step, 0)


def block_kernel(n, groups, names, plans, *refs):
    r = types.SimpleNamespace(**dict(zip(names, refs)))
    feats, cot, basis = r.feats, r.cot, r.basis
    src_ref, tgt_ref = r.src, r.tgt
    z_one, hidden, table, acc = r.z_one, r.hidden, r.table, r.acc
    edges, dim = feats.shape
    width = r.down.shape[1]
    trips = src_ref.shape[1]
    subs = edges // SUB
    half = n // 2
    scale = math.sqrt(0.5)
    me = lax.axis_index("graph")
    tile = min(TILE, trips)
    tiles = trips // tile

    spare = [0]

    def take(count):
        low = spare[0]
        spare[0] += count
        return lambda i: r.sends.at[low + i]

    def total(name):
        large, count = plans[name]
        return total_steps(
            n,
            groups,
            large,
            getattr(r, name + "_in"),
            getattr(r, name + "_out"),
            [getattr(r, name + str(i)) for i in range(count)],
            take(flag_count(n, groups, large)),
            getattr(r, name + "_recv"),
        )

    loads = {}
    for i, name in enumerate(LOADED):
        loads[name] = pltpu.make_async_copy(getattr(r, name + "_far"), getattr(r, name), r.loads.at[i])
        loads[name].start()
    greet_all(n, groups)
    cuts = pieces(r.pair.shape[0])
    early = Gather(
        n,
        [r.pair.at[rows] for rows in cuts] + [r.down, r.wb],
        [r.w_pair.at[:, rows] for rows in cuts] + [r.w_down, r.w_basis],
        r.sends,
        0,
        r.early_recv,
    )
    late = Gather(
        n,
        (r.up, r.first, r.second),
        (r.w_up, r.w_first, r.w_second),
        r.sends,
        early.count * half * 3,
        r.late_recv,
    )
    early.start()
    w_pair = r.w_pair
    for k in range(1, half):
        early.hop(k)
    late.start()
    for k in range(half):
        early.across(k)
    loads["feats"].wait()
    down_own = r.down_own
    f_send, f_recv = r.fwd_send, r.fwd_recv
    ahead = []
    for c in range(subs):
        rows = slice(c * SUB, (c + 1) * SUB)
        value = dot(feats[rows, :], whole(w_pair), NN)
        sig = sigmoid(value)
        act = (value * sig).astype(BF16)
        hidden[rows, :] = act
        down_own[c] = dot(whole(r.w_down), act, ((0,), (1,))).astype(BF16)
        table[me, :, rows] = down_own[c]
        ahead.append([])
        for k in range(1, groups):
            cp = remote(
                down_own.at[c],
                table.at[me, :, rows],
                f_send.at[k - 1, c],
                f_recv.at[k - 1, c],
                {"graph": (me + k) % groups},
            )
            cp.start()
            ahead[c].append(cp)
        z_one[rows, :] = slope_of(value, sig)
    acc[...] = jnp.zeros_like(acc)
    w_basis = whole(r.w_basis)
    din = r.din
    reach = edges // PASSES
    for name in ("basis", "src", "tgt"):
        loads[name].wait()

    def gather_tile(part, i, carry):
        spot = pl.ds(pl.multiple_of(i * tile, tile), tile)
        src = src_ref[:, spot]
        owner = src // edges
        cols = slice(part * reach, (part + 1) * reach)
        stack = dot(
            table[:, :, cols].reshape(groups * width, reach),
            one_hot(reach, src - owner * edges - part * reach),
            NN,
        )
        down_in = pick(stack, owner, groups, width)
        if part > 0:
            down_in = down_in + din[:, spot].astype(F32)
        din[:, spot] = down_in.astype(BF16)
        if part == PASSES - 1:
            tgt = tgt_ref[:, spot]
            coeff = dot(w_basis, basis[:, spot], TN)
            high = tgt // SUB
            acc[...] += dot(
                place(down_in * coeff, high, subs), one_hot(SUB, tgt - high * SUB), NT
            )
        return carry

    units = PASSES * tiles
    stops = {max(units * k // half - 1, 0): k for k in range(1, half)}
    for part in range(PASSES):
        for c in range(subs * part // PASSES, subs * (part + 1) // PASSES):
            for cp in ahead[c]:
                cp.wait()
        low = 0
        for unit in range(tiles):
            if part * tiles + unit in stops:
                lax.fori_loop(low, unit, functools.partial(gather_tile, part), 0)
                low = unit
                late.hop(stops[part * tiles + unit])
        lax.fori_loop(low, tiles, functools.partial(gather_tile, part), 0)
    late.across(0)
    agg = r.agg
    for h in range(subs):
        agg[:, h * SUB : (h + 1) * SUB] = acc[h * width : (h + 1) * width, :].astype(BF16)
    for k in range(1, half):
        late.across(k)

    for gather in (early, late):
        gather.drain()
    loads["cot"].wait()
    mixed, inner = r.mixed, r.inner
    slope_two, slope_three = r.slope_two, r.slope_three
    dz_four, dz_three, dz_two = r.dz_four, r.dz_three, r.dz_two
    block = min(ROWS, edges)

    def outward(rows):
        value = dot(agg[:, rows], whole(r.w_up), TN)
        sig = sigmoid(value)
        act = (value * sig).astype(BF16)
        mixed[rows, :] = act
        slope_two[rows, :] = slope_of(value, sig)
        value = dot(act, whole(r.w_first), NN)
        sig = sigmoid(value)
        act = (value * sig).astype(BF16)
        inner[rows, :] = act
        slope_three[rows, :] = slope_of(value, sig)
        value = dot(act, whole(r.w_second), NN)
        slope = slope_of(value, sigmoid(value))
        dz_four[rows, :] = (scale * cot[rows, :].astype(F32) * slope).astype(BF16)

    by_tile(edges, block, outward)
    spread(r.second_in, dot(inner[...], dz_four[...], TN))
    second = total("second")
    next(second)

    def inward(rows):
        value = dot(dz_four[rows, :], whole(r.w_second), NT) * slope_three[rows, :]
        dz_three[rows, :] = value.astype(BF16)

    by_tile(edges, block, inward)
    next(second)
    spread(r.first_in, dot(mixed[...], dz_three[...], TN))
    first = total("first")
    next(first)
    dagg = r.dagg

    def through(rows):
        value = scale * cot[rows, :].astype(F32) + dot(
            dz_three[rows, :], whole(r.w_first), NT
        )
        value = (value * slope_two[rows, :]).astype(BF16)
        dz_two[rows, :] = value

    by_tile(edges, block, through)
    next(first)
    for h in range(subs):
        rows = slice(h * SUB, (h + 1) * SUB)
        dagg[h * width : (h + 1) * width, :] = dot(
            whole(r.w_up), dz_two[rows, :], NT
        ).astype(BF16)
    spread(r.up_in, dot(agg[...], dz_two[...], NN))
    up = total("up")
    next(up)

    placed, basis_sum = r.placed, r.basis_sum
    basis_sum[...] = jnp.zeros_like(basis_sum)

    def spread_tile(spot):
        src = src_ref[:, spot]
        tgt = tgt_ref[:, spot]
        owner = src // edges
        high = tgt // SUB
        dagg_out = pick(dot(dagg[...], one_hot(SUB, tgt - high * SUB), NN), high, subs, width)
        dcoeff = (dagg_out * din[:, spot].astype(F32)).astype(BF16)
        basis_sum[...] += dot(basis[:, spot], dcoeff, NT)
        coeff = dot(w_basis, basis[:, spot], TN)
        placed[:, spot] = place(dagg_out * coeff, owner, groups)

    by_tile(trips, tile, spread_tile)
    next(second)
    next(up)
    basis_plan = total("basis")
    spread(r.basis_in, basis_sum[...])
    next(basis_plan)
    parts, landed = r.parts, r.landed
    b_send, b_recv = take((groups - 1) * subs), r.bwd_recv
    back = []
    chunk_sum = r.chunk_sum
    calls = {1: (second, first, up, basis_plan, basis_plan)}
    for c in range(subs):
        chunk_sum[...] = jnp.zeros_like(chunk_sum)

        def scatter_tile(spot):
            src = src_ref[:, spot]
            spots = src - src // edges * edges - c * SUB
            chunk_sum[...] += dot(placed[:, spot], one_hot(SUB, spots), NT)

        by_tile(trips, min(SPAN, trips), scatter_tile)
        back.append([])
        for g in range(groups):
            parts[g, c] = chunk_sum[g * width : (g + 1) * width, :].astype(BF16)
        for k in range(1, groups):
            peer = (me + k) % groups
            cp = remote(
                parts.at[peer, c], landed.at[k, c], b_send((k - 1) * subs + c), b_recv.at[k - 1, c], {"graph": peer}
            )
            cp.start()
            back[c].append(cp)
        for steps in calls.get(c, ()):
            next(steps)
    for steps in (first, up, basis_plan):
        next(steps)
    ddown, dz_one, pair_sum = r.ddown, r.dz_one, r.pair_sum
    cols = dim // 2
    for c in range(subs):
        for cp in back[c]:
            cp.wait()
        value = parts[me, c].astype(F32)
        for k in range(1, groups):
            value = value + landed[k, c].astype(F32)
        value = value.astype(BF16)
        rows = slice(c * SUB, (c + 1) * SUB)
        ddown[:, rows] = value
        slope = z_one[rows, :]
        dz_one[rows, :] = (dot(value, whole(r.w_down), ((0,), (1,))) * slope).astype(BF16)
        if c < subs - 1:
            value = dot(feats[rows, :], dz_one[rows, :], TN)
            pair_sum[...] = value if c == 0 else pair_sum[...] + value
    last = slice(edges - SUB, edges)
    for name, part in (("pair_a", slice(0, cols)), ("pair_b", slice(cols, dim))):
        value = dot(feats[last, :], dz_one[last, part], TN)
        if subs > 1:
            value = value + pair_sum[:, part]
        spread(getattr(r, name + "_in"), value)
        if name == "pair_a":
            pair_a = total("pair_a")
            next(pair_a)
    pair_b = total("pair_b")
    next(pair_b)
    next(pair_a)
    spread(r.down_grad_in, dot(hidden[...], ddown[...], ((0,), (1,))))
    down_plan = total("down_grad")
    next(down_plan)
    next(pair_b)
    edge = r.edge

    def input_grad(rows):
        edge[rows, :] = dot(dz_one[rows, :], whole(w_pair), NT).astype(BF16)

    by_tile(edges // 2, block // 2, input_grad)
    next(down_plan)
    next(down_plan)
    next(pair_a)
    next(pair_b)
    by_tile(
        edges // 2, block // 2, lambda rows: input_grad(pl.ds(rows.start + edges // 2, rows.size))
    )
    next(down_plan)
    next(pair_a)
    next(pair_b)
    for steps in (second, first, up, basis_plan, pair_a, pair_b, down_plan):
        for _ in steps:
            pass


def on_device(
    edge_feats,
    cotangent,
    angle_basis,
    source_edge,
    target_edge,
    pair_weight,
    down_weight,
    basis_weight,
    up_weight,
    res_first,
    res_second,
):
    n = lax.axis_size("dp")
    groups = lax.axis_size("graph")
    edges, dim = edge_feats.shape
    width = down_weight.shape[1]
    trips = source_edge.shape[0]
    subs = edges // SUB
    names, shapes = [], []

    def hold(name, *shape, kind=BF16):
        names.append(name)
        shapes.append(pltpu.VMEM(shape, kind))

    def flags(name, *shape):
        names.append(name)
        shapes.append(pltpu.SemaphoreType.DMA(shape))

    args = dict(
        feats=edge_feats,
        cot=cotangent,
        basis=angle_basis,
        src=source_edge.reshape(1, -1),
        tgt=target_edge.reshape(1, -1),
        pair=pair_weight,
        down=down_weight,
        wb=basis_weight,
        up=up_weight,
        first=res_first,
        second=res_second,
    )
    outs = {"edge": jax.ShapeDtypeStruct((edges, dim), BF16)}
    plans, used = {}, []

    def plan(name, rows, cols, large, kind=BF16):
        lead = (2, n // 2, groups) if large else (2, n // 2)
        shape = lead + (rows // (n * groups if large else n), cols)
        landing, scratch = total_parts(n, groups, shape, large, kind)
        outs[name + "_out"] = landing
        hold(name + "_in", *shape, kind=kind)
        for i, extra in enumerate(scratch):
            names.append(name + str(i))
            shapes.append(extra)
        size = flag_count(n, groups, large)
        flags(name + "_recv", size)
        plans[name] = (large, len(scratch))
        used.append(size)

    plan("pair_a", dim, dim // 2, True)
    plan("pair_b", dim, dim // 2, True)
    plan("down_grad", dim, width, False)
    plan("basis", angle_basis.shape[0], width, False, F32)
    plan("up", width, dim, False)
    plan("first", dim, dim, True)
    plan("second", dim, dim, True)
    for name, shard in (
        ("w_pair", pair_weight),
        ("w_down", down_weight),
        ("w_basis", basis_weight),
        ("w_up", up_weight),
        ("w_first", res_first),
        ("w_second", res_second),
    ):
        hold(name, n, *shard.shape)
    for name in ("z_one", "slope_two", "slope_three"):
        hold(name, edges, dim, kind=F32)
    for name in ("hidden", "mixed", "inner", "dz_four", "dz_three", "dz_two", "dz_one"):
        hold(name, edges, dim)
    hold("table", groups, width, edges)
    hold("down_own", subs, width, SUB)
    hold("acc", subs * width, SUB, kind=F32)
    hold("din", width, trips)
    hold("agg", width, edges)
    hold("dagg", subs * width, SUB)
    hold("placed", groups * width, trips)
    hold("basis_sum", angle_basis.shape[0], width, kind=F32)
    hold("chunk_sum", groups * width, SUB, kind=F32)
    hold("parts", groups, subs, width, SUB)
    hold("landed", groups, subs, width, SUB)
    hold("ddown", width, edges)
    count = len(pieces(pair_weight.shape[0])) + 2
    flags("early_recv", n, count)
    flags("late_recv", n, 3)
    used.append((groups - 1) * subs)
    flags("sends", max(n // 2 * 3 * (count + 3), sum(used)))
    for name in ("fwd_send", "fwd_recv", "bwd_recv"):
        flags(name, groups - 1, subs)
    hold("pair_sum", dim, dim, kind=F32)
    for name in LOADED:
        hold(name, *args[name].shape, kind=args[name].dtype)
    names.append("loads")
    shapes.append(pltpu.SemaphoreType.DMA((len(LOADED),)))
    firsts = [name + "_far" if name in LOADED else name for name in args]
    results = pl.pallas_call(
        functools.partial(block_kernel, n, groups, firsts + list(outs) + names, plans),
        out_shape=list(outs.values()),
        in_specs=[ANY if name in LOADED else VM for name in args],
        out_specs=[VM] * len(outs),
        scratch_shapes=shapes,
        compiler_params=pltpu.CompilerParams(collective_id=0, has_side_effects=True),
        name="block",
    )(*args.values())
    got = dict(zip(outs, results))
    return write_grads(got, groups)


def write_kernel(ins, outs, *refs):
    landed = dict(zip(ins, refs))
    for name, out in zip(outs, refs[len(ins) :]):
        if name == "edge":
            out[...] = landed["edge"][...]
            continue
        col = 0
        for part in (name,) if name in landed else (name + "_a", name + "_b"):
            item = landed[part]
            groups, rows, cols = item.shape
            spot = slice(col, col + cols)
            col += cols
            if name in SHARED:
                value = item[0].astype(F32)
                for g in range(1, groups):
                    value = value + item[g].astype(F32)
                out[:, spot] = value
            else:
                for g in range(groups):
                    out[g * rows : (g + 1) * rows, spot] = item[g].astype(F32)


SHARED = ("down_grad", "basis", "up")


def write_grads(got, groups):
    got = {name.removesuffix("_out"): item for name, item in got.items()}
    dim = got["edge"].shape[1]
    outs = {"edge": jax.ShapeDtypeStruct(got["edge"].shape, BF16)}
    for name in ("pair", "down_grad", "basis", "up", "first", "second"):
        item = got[name] if name in got else got[name + "_a"]
        rows = item.shape[1] * (1 if name in SHARED else groups)
        cols = item.shape[2] if name in got else dim
        outs[name] = jax.ShapeDtypeStruct((rows, cols), F32)
    return tuple(
        pl.pallas_call(
            functools.partial(write_kernel, list(got), list(outs)),
            out_shape=list(outs.values()),
            in_specs=[VM] * len(got),
            out_specs=[VM] * len(outs),
            name="write_grads",
        )(*got.values())
    )


def solution(mesh):
    return jax.shard_map(
        on_device,
        mesh=mesh,
        in_specs=(
            P(("dp", "graph"), None),
            P(("dp", "graph"), None),
            P(None, ("dp", "graph")),
            P(("dp", "graph")),
            P(("dp", "graph")),
            P("dp", None),
            P("dp", None),
            P("dp", None),
            P("dp", None),
            P("dp", None),
            P("dp", None),
        ),
        out_specs=(
            P(("dp", "graph"), None),
            P("dp", None),
            P("dp", None),
            P("dp", None),
            P("dp", None),
            P("dp", None),
            P("dp", None),
        ),
        check_vma=False,
    )
```
